32 devices in a mesh: freq: 2 (over x), facet: 16 (over z, y, core).
Axes of the slice: x: 2, y: 2, z: 4, core: 2. Of those that a mesh axis runs over, the one named last changes fastest.
Arguments:
- model_image: float32 [128, 2048], P('facet'), may hold values from -6 to 6
- visibilities: float32 [2, 8192], P(None, ('freq', 'facet')), may hold values from -6 to 6
- kernel_u: float32 [16, 8192], P(None, ('freq', 'facet')), may hold values from -1.5 to 1.5
- kernel_v: float32 [16, 8192], P(None, ('freq', 'facet')), may hold values from -1.5 to 1.5
- owners: int32 [8192, 1], P(('freq', 'facet')), may hold values from 0 to 15; in each aligned block of 256 rows (0 to 255, 256 to 511, ...) at most 64 rows name the same one
- offsets: int32 [2, 8192], P(None, ('freq', 'facet')), may hold values from 0 to 48
- corners: int32 [2, 16, 2], P('freq'), may hold values from -8192 to 8128
Outputs:
- model_out: float32 [128, 2048], P('facet')
- residual_rows: float32 [2, 8192], P(None, ('freq', 'facet'))
The draws below stay inside these ranges and needn't reach their ends.
Inputs may be any that keep to these rules, and one draw needn't show every extreme that they name: `owners`: within each device's 256 rows, at most 64 rows name one owner, a bound that some block reaches of them.
All inputs are finite; a program needn't handle non-finite values.
Results may differ from the reference program's by a relative error of at most 0.0045.
Values sent between devices are 32-bit elements; how exact they have to be, the bound alone decides.
No kernel may reach another device: no remote copies, remote signals or barrier semaphores. Data moves between devices by JAX's collectives and lax.ppermute only.
A program may use at most 64 MiB of HBM per device.

```python
import math
import jax
import jax.numpy as jnp
import numpy as np
from jax import lax

GRID = 16384
FACET = 2048
FROWS = 8
SUB = 64
SUPPORT = 16
CYCLES = 2
V_DEV = 256
CAP = 64
VIS = 8192
N_FREQ = 2
N_FACET = 16


def set_ends(drawn, rng, low, largest):
    longest = drawn.shape.index(max(drawn.shape))
    spots = []
    for shift in (0, 1):
        where = [jax.random.randint(jax.random.fold_in(rng, axis), (), 0, length) for axis, length in enumerate(drawn.shape)]
        where[longest] = (where[longest] + shift) % drawn.shape[longest]
        spots.append(tuple(where))
    return drawn.at[spots[0]].set(low).at[spots[1]].set(largest)


def steps_of(rng, extent, split, low, largest):
    loudness, own = 1.0, jax.random.fold_in(rng, 6)
    for dim, parts in split:
        steps = jnp.exp(jax.random.uniform(jax.random.fold_in(own, dim), (parts,), jnp.float32, low / len(split), largest / len(split)))
        loudness = loudness * jnp.repeat(steps, extent[dim] // parts).reshape([-1 if axis == dim else 1 for axis in range(len(extent))])
    return loudness


def deal_out(rng, own, number, rows, count, top, reach, slope):
    sequence = jax.random.permutation(rng, count)
    heavy_load, usual = portions_of(count, rows * top, reach, slope, True), portions_of(count, rows * top, reach, slope, False)
    places = jnp.arange(count)

    def named(sizes, rotation):
        used = int((sizes > 0).sum())
        fixed = max(1, used // 4)
        passed = fixed + (places - fixed + rotation * (used - fixed)) % max(1, count - fixed)
        return jnp.zeros((count,), jnp.int32).at[sequence[jnp.where(places < fixed, places, passed)]].set(jnp.asarray(sizes, jnp.int32))

    sizes = jnp.where(number % 4 == 0, named(heavy_load, number // 4), named(usual, number - number // 4 - 1))
    mixed = jax.random.permutation(jax.random.fold_in(own, 3), count)
    source_of, taker = mixed[0:count // 2 * 2:2], mixed[1:count // 2 * 2:2]
    slack = jnp.minimum(sizes[source_of] - 1, reach - sizes[taker]) // 2
    slack = jnp.where((source_of == sequence[0]) | (taker == sequence[0]) | (sizes[taker] == 0), 0, jnp.maximum(slack, 0))
    passed = jax.random.randint(jax.random.fold_in(own, 4), (count // 2,), 0, 1 << 20) % (slack + 1)
    sizes = sizes.at[source_of].add(-passed).at[taker].add(passed)
    items = jnp.searchsorted(jnp.cumsum(sizes), jnp.arange(rows * top), side="right").astype(jnp.int32)
    grid = items.reshape(top, rows).T
    grid = grid[jax.random.permutation(jax.random.fold_in(own, 1), rows)]
    rotation = jax.random.randint(jax.random.fold_in(own, 2), (rows, 1), 0, top)
    return jnp.take_along_axis(grid, (jnp.arange(top)[None, :] + rotation) % top, axis=1)


def portions_of(number_of, total, reach, slope, full):
    portions = [(1 << 20) // math.isqrt(rank ** slope) + 1 for rank in range(1, number_of + 1)]
    largest = reach if full else min(reach, max(-(-total // number_of), total * portions[0] // sum(portions)))
    least = 1 if total - largest >= number_of - 1 else 0
    given, rest = [largest] + [least] * (number_of - 1), total - largest - least * (number_of - 1)
    while rest > 0:
        candidates = [i for i in range(1, number_of) if given[i] < largest] or [i for i in range(1, number_of) if given[i] < reach]
        mass, remaining = sum([portions[i] for i in candidates]), rest
        for i in candidates:
            extra = min(reach - given[i], max(1, remaining * portions[i] // mass), rest)
            given[i] = given[i] + extra
            rest = rest - extra
    return np.array(given)


def noise(rng, dims, deviation, most, shards=(), kind=jnp.bfloat16):
    result = deviation * jax.random.normal(rng, dims, jnp.float32)
    if shards:
        result = result * steps_of(rng, dims, shards, -0.22, 0.18)
    return jnp.clip(result, -most, most).astype(kind)


def setup_inputs(seed: int = 0) -> dict:
    key_list = jax.random.split(jax.random.key(seed), 8)
    model_image = noise(key_list[0], (N_FACET * FROWS, FACET), 1.0, 6.0, ((0, 16),), jnp.float32)
    visibilities = noise(key_list[1], (2, VIS), 1.0, 6.0, ((1, 32),), jnp.float32)
    kernel_u = noise(key_list[2], (SUPPORT, VIS), 0.25, 1.5, ((1, 32),), jnp.float32)
    kernel_v = noise(key_list[3], (SUPPORT, VIS), 0.25, 1.5, ((1, 32),), jnp.float32)
    owners_keys = jax.random.split(jax.random.fold_in(key_list[4], 1), VIS // V_DEV)
    owners_turns = jax.random.permutation(jax.random.fold_in(key_list[4], 3), VIS // V_DEV)
    owners = jax.vmap(lambda own, number: deal_out(jax.random.fold_in(key_list[4], 2), own, number, V_DEV, N_FACET, 1, CAP, 2))(owners_keys, owners_turns).reshape((VIS, 1))
    offsets = set_ends(jax.random.randint(key_list[5], (2, VIS), 0, SUB - SUPPORT + 1), jax.random.fold_in(key_list[5], 1), 0, SUB - SUPPORT).astype(jnp.int32)
    corners = set_ends(jax.random.randint(key_list[6], (N_FREQ, N_FACET, 2), -(GRID // 2), GRID // 2 - SUB + 1), jax.random.fold_in(key_list[6], 1), -(GRID // 2), (GRID // 2 - SUB + 1) - 1).astype(jnp.int32)
    return dict(model_image=model_image, visibilities=visibilities, kernel_u=kernel_u, kernel_v=kernel_v, owners=owners, offsets=offsets, corners=corners)


exact_products = lax.Precision.HIGHEST
GAIN_STEP = 0.5

def phase_pair(freq_index, position):
    angle_value = jnp.mod(freq_index * position, GRID).astype(jnp.float32) * (2.0 * math.pi / GRID)
    return (jnp.cos(angle_value), jnp.sin(angle_value))

def column_table():
    columns = jnp.arange(FACET, dtype=jnp.int32)
    frequency = jnp.arange(SUB, dtype=jnp.int32)
    cos_t, sin_t = phase_pair(frequency[None, :], columns[:, None])
    return jnp.concatenate([cos_t, sin_t], axis=1)

def make_back(col_table):
    cos_t = col_table[:, :SUB].T
    sin_t = col_table[:, SUB:].T
    upper = jnp.concatenate([cos_t, sin_t], axis=1)
    lower = jnp.concatenate([-sin_t, cos_t], axis=1)
    return jnp.concatenate([upper, lower], axis=0)

def forward_part(images, facet_ids, u_start, v_start, col_table):
    amount = images.shape[0]
    columns = jnp.arange(FACET, dtype=jnp.int32)
    cos_u, sin_u = phase_pair(u_start, columns)
    real_mod = (images * cos_u).reshape(amount * FROWS, FACET).astype(jnp.bfloat16)
    imag_mod = (-images * sin_u).reshape(amount * FROWS, FACET).astype(jnp.bfloat16)
    table_half = col_table.astype(jnp.bfloat16)
    real_prod = jnp.dot(real_mod, table_half, preferred_element_type=jnp.float32).reshape(amount, FROWS, 2 * SUB)
    imag_prod = jnp.dot(imag_mod, table_half, preferred_element_type=jnp.float32).reshape(amount, FROWS, 2 * SUB)
    col_re = real_prod[..., :SUB] + imag_prod[..., SUB:]
    col_im = imag_prod[..., :SUB] - real_prod[..., SUB:]
    frequency = jnp.arange(SUB, dtype=jnp.int32)
    x_start = facet_ids % (GRID // FACET) * FACET - GRID // 2
    cos_x, sin_x = phase_pair(u_start + frequency[None, :], x_start[:, None])
    shift_re = col_re * cos_x[:, None, :] + col_im * sin_x[:, None, :]
    shift_im = col_im * cos_x[:, None, :] - col_re * sin_x[:, None, :]
    y_pos = (facet_ids // (GRID // FACET) * FACET - GRID // 2)[:, None] + jnp.arange(FROWS, dtype=jnp.int32)[None, :]
    cosine_vertical, sine_vertical = phase_pair(v_start + frequency[:, None, None], y_pos[None])
    grid_re = jnp.einsum('bfr,fra->ba', cosine_vertical, shift_re, precision=exact_products) + jnp.einsum('bfr,fra->ba', sine_vertical, shift_im, precision=exact_products)
    grid_im = jnp.einsum('bfr,fra->ba', cosine_vertical, shift_im, precision=exact_products) - jnp.einsum('bfr,fra->ba', sine_vertical, shift_re, precision=exact_products)
    return jnp.stack([grid_re, grid_im], axis=1)

def forward_sum(images, facet_ids, u_start, v_start, col_table):
    amount = images.shape[0]
    blocking = math.gcd(amount, 8)

    def accumulate(running, pieces):
        return (running + forward_part(pieces[0], pieces[1], u_start, v_start, col_table), None)
    sectioned = images.reshape(amount // blocking, blocking, FROWS, FACET)
    sectioned_ids = facet_ids.reshape(amount // blocking, blocking)
    running, unused = lax.scan(accumulate, jnp.zeros((SUB, 2, SUB), jnp.float32), (sectioned, sectioned_ids))
    return running

def adjoint_part(blocks, u_starts, v_starts, facet_here, back_table):
    amount = blocks.shape[0]
    frequency = jnp.arange(SUB, dtype=jnp.int32)
    y_pos = facet_here // (GRID // FACET) * FACET - GRID // 2 + jnp.arange(FROWS, dtype=jnp.int32)
    cosine_vertical, sine_vertical = phase_pair(v_starts[:, None, None] + frequency[None, :, None], y_pos[None, None, :])
    kernel_real = blocks[:, :, 0, :]
    kernel_imaginary = blocks[:, :, 1, :]
    row_real = jnp.einsum('gil,gik->glk', cosine_vertical, kernel_real, precision=exact_products) - jnp.einsum('gil,gik->glk', sine_vertical, kernel_imaginary, precision=exact_products)
    row_imaginary = jnp.einsum('gil,gik->glk', cosine_vertical, kernel_imaginary, precision=exact_products) + jnp.einsum('gil,gik->glk', sine_vertical, kernel_real, precision=exact_products)
    x_start = facet_here % (GRID // FACET) * FACET - GRID // 2
    cos_x, sin_x = phase_pair(u_starts[:, None] + frequency[None, :], x_start)
    shift_re = row_real * cos_x[:, None, :] - row_imaginary * sin_x[:, None, :]
    shift_im = row_imaginary * cos_x[:, None, :] + row_real * sin_x[:, None, :]
    joined = jnp.concatenate([shift_re, shift_im], axis=2).reshape(amount * FROWS, 2 * SUB).astype(jnp.bfloat16)
    both = jnp.dot(joined, back_table.astype(jnp.bfloat16), preferred_element_type=jnp.float32).reshape(amount, FROWS, 2 * FACET)
    columns = jnp.arange(FACET, dtype=jnp.int32)
    cos_u, sin_u = phase_pair(u_starts[:, None], columns[None, :])
    return lax.optimization_barrier(jnp.sum(both[..., :FACET] * cos_u[:, None, :] - both[..., FACET:] * sin_u[:, None, :], axis=0))

def adjoint_sum(blocks, corner_list, facet_here, back_table):
    amount = blocks.shape[0]
    blocking = math.gcd(amount, 8)

    def accumulate(running, pieces):
        return (running + adjoint_part(pieces[0], pieces[1][:, 0], pieces[1][:, 1], facet_here, back_table), None)
    sectioned = blocks.reshape(amount // blocking, blocking, SUB, 2, SUB)
    starts = corner_list.reshape(amount // blocking, blocking, 2)
    running, unused = lax.scan(accumulate, jnp.zeros((FROWS, FACET), jnp.float32), (sectioned, starts))
    return running

def slot_positions(owner_ids, capacity, owner_count):
    owner_hits = (owner_ids[:, None] == jnp.arange(owner_count, dtype=jnp.int32)[None, :]).astype(jnp.int32)
    before = jnp.cumsum(owner_hits, axis=0) - owner_hits
    return owner_ids * capacity + lax.optimization_barrier(jnp.sum(before * owner_hits, axis=1))

def place_kernel(kernel, offset_row):
    row_ids = jnp.arange(SUB, dtype=jnp.int32)[:, None]
    placed = jnp.zeros((SUB, kernel.shape[1]), jnp.float32)
    for kernel_tap in range(SUPPORT):
        placed = placed + jnp.where(row_ids == offset_row[None, :] + kernel_tap, kernel[kernel_tap][None, :], 0.0)
    return placed

def predict_rows(grid_block, kern_u, kern_v):
    partial_rows = jnp.einsum('bpa,ar->bpr', grid_block, kern_u, precision=exact_products)
    return lax.optimization_barrier(jnp.sum(kern_v[:, None, :] * partial_rows, axis=0))

def grid_rows(residual, kern_u, kern_v):
    return jnp.einsum('br,par->bpa', kern_v, residual[:, None, :] * kern_u[None], precision=exact_products)

def owner_step(grid_block, arrived):
    observed = arrived[0:2]
    kern_u = place_kernel(arrived[2:2 + SUPPORT], arrived[2 + 2 * SUPPORT].astype(jnp.int32))
    kern_v = place_kernel(arrived[2 + SUPPORT:2 + 2 * SUPPORT], arrived[3 + 2 * SUPPORT].astype(jnp.int32))
    residual = observed - predict_rows(grid_block, kern_u, kern_v)
    return (residual, grid_rows(residual, kern_u, kern_v))

def reference(model_image, visibilities, kernel_u, kernel_v, owners, offsets, corners):
    scale = 1.0 / math.sqrt(N_FACET * FROWS * FACET)
    owner_ids = owners[:, 0].reshape(N_FREQ, N_FACET, V_DEV)
    payload = jnp.concatenate([visibilities, kernel_u, kernel_v, offsets.astype(jnp.float32)], axis=0)
    feature_rows = payload.shape[0]
    per_device = payload.reshape(feature_rows, N_FREQ, N_FACET, V_DEV).transpose(1, 2, 0, 3)
    slot_index = jax.vmap(jax.vmap(lambda owner_row: slot_positions(owner_row, CAP, N_FACET)))(owner_ids)

    def fill_slots(device_rows, device_slots):
        return jnp.zeros((feature_rows, N_FACET * CAP), jnp.float32).at[:, device_slots].set(device_rows)
    send_buffer = jax.vmap(jax.vmap(fill_slots))(per_device, slot_index)
    arrived = send_buffer.reshape(N_FREQ, N_FACET, feature_rows, N_FACET, CAP).transpose(0, 3, 2, 1, 4)
    arrived = arrived.reshape(N_FREQ * N_FACET, feature_rows, N_FACET * CAP)
    col_table = column_table()
    back_table = make_back(col_table)
    flat_corners = corners.reshape(N_FREQ * N_FACET, 2)
    facet_list = jnp.arange(N_FACET, dtype=jnp.int32)
    current = model_image
    residual = jnp.zeros((N_FREQ * N_FACET, 2, N_FACET * CAP), jnp.float32)
    for major_cycle in range(CYCLES):
        images = current.reshape(N_FACET, FROWS, FACET)
        grids = lax.map(lambda corner: scale * forward_sum(images, facet_list, corner[0], corner[1], col_table), flat_corners)
        residual, gridded = lax.map(lambda pieces: owner_step(pieces[0], pieces[1]), (grids, arrived))
        dirty_image = lax.map(lambda facet_here: scale * adjoint_sum(gridded, flat_corners, facet_here, back_table), facet_list)
        current = current + GAIN_STEP * dirty_image.reshape(N_FACET * FROWS, FACET)
    returned = residual.reshape(N_FREQ, N_FACET, 2, N_FACET, CAP).transpose(0, 3, 2, 1, 4)
    returned = returned.reshape(N_FREQ, N_FACET, 2, N_FACET * CAP)
    picked = jax.vmap(jax.vmap(lambda device_rows, device_slots: device_rows[:, device_slots]))(returned, slot_index)
    residual_rows = picked.transpose(2, 0, 1, 3).reshape(2, VIS)
    return (current, residual_rows)
```

```python
import math

import jax
import jax.numpy as jnp
from jax import lax
from jax.experimental import pallas as pl
from jax.experimental.pallas import tpu as pltpu
from jax.sharding import PartitionSpec as P

GRID = 16384
FACET = 2048
FROWS = 8
SUB = 64
SUPPORT = 16
LANES = 128
ACROSS = GRID // FACET
GROUPS = 5
GAIN_STEP = 0.5

F32 = jnp.float32
BF16 = jnp.bfloat16
I32 = jnp.int32
exact_products = lax.Precision.HIGHEST


def iota(shape, dim):
    return lax.broadcasted_iota(I32, shape, dim)


def phase_pair(index):
    moved = index + GRID // 8
    quadrant = (moved >> 12) & 3
    angle = ((moved & (GRID // 4 - 1)) - GRID // 8).astype(F32) * (2.0 * math.pi / GRID)
    sq = angle * angle
    sin_p = angle * (1.0 + sq * (-1.0 / 6 + sq * (1.0 / 120 + sq * (-1.0 / 5040 + sq * (1.0 / 362880)))))
    cos_p = 1.0 + sq * (-0.5 + sq * (1.0 / 24 + sq * (-1.0 / 720 + sq * (1.0 / 40320))))
    swap = (quadrant & 1) == 1
    cos_v = jnp.where(swap, sin_p, cos_p)
    sin_v = jnp.where(swap, cos_p, sin_p)
    cos_v = jnp.where((quadrant == 1) | (quadrant == 2), -cos_v, cos_v)
    sin_v = jnp.where(quadrant >= 2, -sin_v, sin_v)
    return cos_v, sin_v


def phase_rows(freq):
    cos_v, sin_v = phase_pair(freq * iota(freq.shape, 1))
    turn_c, turn_s = phase_pair(freq * LANES)
    cos_l, sin_l = [cos_v], [sin_v]
    while len(cos_l) < FACET // LANES:
        more_c = [c * turn_c - s * turn_s for c, s in zip(cos_l, sin_l)]
        more_s = [s * turn_c + c * turn_s for c, s in zip(cos_l, sin_l)]
        cos_l, sin_l = cos_l + more_c, sin_l + more_s
        turn_c, turn_s = turn_c * turn_c - turn_s * turn_s, 2.0 * turn_c * turn_s
    return jnp.concatenate(cos_l, axis=1), jnp.concatenate(sin_l, axis=1)


def dot_nt(left, right, precision=None):
    return lax.dot_general(
        left, right, (((1,), (1,)), ((), ())), precision=precision, preferred_element_type=F32
    )


def dot_nn(left, right, precision=None):
    return lax.dot_general(
        left, right, (((1,), (0,)), ((), ())), precision=precision, preferred_element_type=F32
    )


def layout_of(cap):
    lane_groups = LANES // cap
    row_blocks = -(-GROUPS // lane_groups)
    return lane_groups, row_blocks, FROWS + 8 * row_blocks


def slot_parts(owner_row, count):
    rows = owner_row.shape[1]
    hits = (iota((count, rows), 0) == owner_row).astype(F32)
    earlier = (iota((rows, rows), 0) < iota((rows, rows), 1)).astype(F32)
    before = dot_nn(hits.astype(BF16), earlier.astype(BF16))
    return hits, jnp.sum(before * hits, axis=0, keepdims=True).astype(I32)


def splat_rows(corner_ref, target_ref, start, count, step):
    for s in range(count):
        target_ref[pl.ds(start + s, 1), :] = jnp.full((1, LANES), corner_ref[step * s], I32)


def send_kernel(
    corner_ref, owner_ref, vis_ref, ku_ref, kv_ref, off_ref, image_ref,
    send_ref, table_ref, freq_ref, mod_ref, *, count, cap,
):
    lane_groups, row_blocks, piece = layout_of(cap)
    facet = lax.axis_index("facet")
    x_start = facet % ACROSS * FACET - GRID // 2
    splat_rows(corner_ref, freq_ref, 0, count, 2)
    freq = freq_ref[...]
    cos_t, sin_t = phase_rows(iota((SUB, LANES), 0))
    table = jnp.concatenate([cos_t, sin_t], axis=0).astype(BF16)
    table_ref[...] = table
    cos_u, sin_u = phase_rows(freq)
    image = image_ref[...]
    for s in range(count):
        both = jnp.concatenate([image * cos_u[s : s + 1], -image * sin_u[s : s + 1]], axis=0)
        mod_ref[16 * s : 16 * s + 16, :] = both.astype(BF16)
    prod = dot_nt(mod_ref[...], table)
    lane = iota((FROWS, LANES), 1)
    low = lane < SUB
    cos_x, sin_x = phase_pair((freq + (iota(freq.shape, 1) & (SUB - 1))) * x_start)
    sin_x = jnp.where(iota(freq.shape, 1) < SUB, sin_x, -sin_x)
    for s in range(count):
        real_p = prod[16 * s : 16 * s + 8]
        imag_p = pltpu.roll(prod[16 * s + 8 : 16 * s + 16], SUB, 1)
        col = jnp.where(low, real_p + imag_p, imag_p - real_p)
        send_ref[piece * s : piece * s + FROWS, :] = (
            col * cos_x[s : s + 1] + pltpu.roll(col, SUB, 1) * sin_x[s : s + 1]
        )

    owner_row = owner_ref[...]
    rows = owner_row.shape[1]
    hits, rank = slot_parts(owner_row, count)
    blank = jnp.zeros((4, rows), F32)
    misc = jnp.concatenate([vis_ref[...], off_ref[...].astype(F32), blank], axis=0)
    parts = [ku_ref[0:8, :], ku_ref[8:16, :], kv_ref[0:8, :], kv_ref[8:16, :], misc]
    total = jnp.zeros((count * row_blocks * 8, LANES), F32)
    for group in range(lane_groups):
        mine = parts[group * row_blocks : (group + 1) * row_blocks]
        if not mine:
            continue
        if len(mine) < row_blocks:
            mine = mine + [jnp.zeros((8, rows), F32)] * (row_blocks - len(mine))
        stacked = jnp.concatenate(mine, axis=0)
        masked = jnp.concatenate([stacked * hits[s : s + 1] for s in range(count)], axis=0)
        place = (iota((LANES, rows), 0) == rank + group * cap).astype(F32)
        total = total + dot_nt(masked, place, exact_products)
    for s in range(count):
        send_ref[piece * s + FROWS : piece * (s + 1), :] = total[
            8 * row_blocks * s : 8 * row_blocks * (s + 1)
        ]


def place_kernel(taps, offset):
    low = jnp.concatenate([taps, jnp.zeros((8, LANES), F32)], axis=0)
    for step in (1, 2, 4):
        bit = jnp.broadcast_to((offset & step) != 0, low.shape)
        low = jnp.where(bit, pltpu.roll(low, step, 0), low)
    zero = jnp.zeros((8, LANES), F32)
    blocks = [low[0:8], low[8:16], low[16:24]]
    for step in (1, 2, 4):
        bit = jnp.broadcast_to((offset & (8 * step)) != 0, (8, LANES))
        size = min(len(blocks) + step, SUB // 8)
        wide = blocks + [zero] * (size - len(blocks))
        blocks = [jnp.where(bit, wide[k - step] if k >= step else zero, wide[k]) for k in range(size)]
    return jnp.concatenate(blocks, axis=0)


def predict(column_rows, kern_u, kern_h, vis, scale):
    height = column_rows.shape[0]
    stacked = jnp.concatenate([column_rows[:, :SUB], column_rows[:, SUB:]], axis=0)
    partial = dot_nn(stacked, kern_u, exact_products)
    part_re, part_im = partial[:height], partial[height:]
    h_re, h_im = kern_h[:height], kern_h[height:]
    pred_re = jnp.sum(h_re * part_re - h_im * part_im, axis=0, keepdims=True)
    pred_im = jnp.sum(h_re * part_im + h_im * part_re, axis=0, keepdims=True)
    return vis[0:1] - scale * pred_re, vis[1:2] - scale * pred_im


def grid_rows(res_re, res_im, kern_u, kern_h):
    height = kern_h.shape[0] // 2
    h_re, h_im = kern_h[:height], kern_h[height:]
    spread = jnp.concatenate([h_re * res_re + h_im * res_im, h_re * res_im - h_im * res_re], axis=0)
    rows = dot_nt(spread, kern_u, exact_products)
    return jnp.concatenate([rows[:height], rows[height:]], axis=1)


def first_kernel(
    corner_ref, got_ref, col_ref, ku_ref, kh_ref, vis_ref, rows_ref, own_ref, *, count, cap, groups, scale,
):
    lane_groups, row_blocks, piece = layout_of(cap)
    height = count // ACROSS * FROWS
    v_start = corner_ref[2 * lax.axis_index("facet") + 1]
    sums = []
    for down in range(count // ACROSS):
        total = got_ref[piece * down * ACROSS : piece * down * ACROSS + FROWS, :]
        for across in range(1, ACROSS):
            at = piece * (down * ACROSS + across)
            total = total + got_ref[at : at + FROWS, :]
        sums.append(total)
    columns = jnp.concatenate(sums, axis=0)
    col_ref[...] = columns
    lane_group = iota((8, LANES), 1) // cap
    u_list, v_list, vis_list = [], [], []
    for tile in range(count // lane_groups):
        found = []
        for k in range(GROUPS):
            block, group = k % row_blocks, k // row_blocks
            value = None
            for j in range(lane_groups):
                at = piece * (tile * lane_groups + j) + FROWS + 8 * block
                moved = got_ref[at : at + 8, :]
                shift = (j - group) * cap % LANES
                if shift:
                    moved = pltpu.roll(moved, shift, 1)
                value = moved if value is None else jnp.where(lane_group == j, moved, value)
            found.append(value)
        misc = found[4]
        u_list.append(place_kernel(jnp.concatenate(found[0:2], axis=0), misc[2:3].astype(I32)))
        v_list.append(place_kernel(jnp.concatenate(found[2:4], axis=0), misc[3:4].astype(I32)))
        vis_list.append(misc)
    kern_u = jnp.concatenate(u_list, axis=1)
    kern_v = jnp.concatenate(v_list, axis=1)
    vis = jnp.concatenate(vis_list, axis=1)
    row = iota((height, SUB), 0)
    y_pos = row // FROWS * FACET - GRID // 2 + row % FROWS
    cos_y, sin_y = phase_pair((v_start + iota((height, SUB), 1)) * y_pos)
    kern_h = dot_nn(jnp.concatenate([cos_y, -sin_y], axis=0), kern_v, exact_products)
    ku_ref[...] = kern_u
    kh_ref[...] = kern_h
    vis_ref[...] = vis
    res_re, res_im = predict(columns, kern_u, kern_h, vis, scale)
    rows = grid_rows(res_re, res_im, kern_u, kern_h)
    own_ref[...] = rows
    for d in range(groups * count):
        rows_ref[height * d : height * (d + 1), :] = rows


def group_corner(corner_ref, near_refs, group, groups, index):
    refs = [corner_ref] + list(near_refs)
    back = (lax.axis_index("freq") - group) % groups
    value = refs[0][2 * index]
    for k in range(1, groups):
        value = jnp.where(back == k, refs[k][2 * index], value)
    return value


def second_kernel(*refs, count, cap, groups, scale):
    corner_ref, near_refs = refs[0], refs[1:groups]
    all_ref, own_ref, col_ref, ku_ref, kh_ref, vis_ref, back_ref, sum_ref = refs[groups:]
    lane_groups = LANES // cap
    height = col_ref.shape[0]
    u_start = corner_ref[2 * lax.axis_index("facet")]
    sum_ref[...] = jnp.zeros_like(sum_ref)
    row, col = iota((LANES, LANES), 0), iota((LANES, LANES), 1)
    same = (row < SUB) == (col < SUB)
    row_a, col_a = row & (SUB - 1), col & (SUB - 1)
    sign = jnp.where(col < SUB, 1.0, -1.0)
    half = GRID // 2

    def overlap(d, carry):
        u_other = group_corner(corner_ref, near_refs, d // count, groups, d % count)
        ahead = ((u_start - u_other + half) & (GRID - 1)) - half
        mirror = (-u_start - u_other) & (GRID - 1)

        @pl.when(((ahead > -SUB) & (ahead < SUB)) | (mirror < 2 * SUB - 1))
        def _():
            select = jnp.where(same & (row_a == col_a + ahead), 1.0, 0.0)
            select = select + jnp.where(same & (row_a + col_a == mirror), sign, 0.0)
            block = all_ref[pl.ds(pl.multiple_of(d * height, 8), height), :]
            sum_ref[...] += dot_nn(block, select, exact_products)

        return carry

    lax.fori_loop(0, groups * count, overlap, 0)
    columns = col_ref[...] + (GAIN_STEP * scale * (GRID / 2)) * sum_ref[...]
    kern_u, kern_h = ku_ref[...], kh_ref[...]
    res_re, res_im = predict(columns, kern_u, kern_h, vis_ref[...], scale)
    rows = own_ref[...] + grid_rows(res_re, res_im, kern_u, kern_h)
    res = jnp.concatenate([res_re, res_im, jnp.zeros((6, res_re.shape[1]), F32)], axis=0)
    for s in range(count):
        tile, j = s // lane_groups, s % lane_groups
        block = res[:, LANES * tile : LANES * (tile + 1)]
        if j:
            block = pltpu.roll(block, LANES - j * cap, 1)
        down = s // ACROSS
        for g in range(groups):
            at = 16 * (g * count + s)
            back_ref[at : at + 8, :] = rows[8 * down : 8 * down + 8]
            back_ref[at + 8 : at + 16, :] = block


def image_kernel(*refs, count, groups, scale):
    corner_ref, near_refs = refs[0], refs[1:groups]
    got_ref, table_ref, owner_ref, image_ref, out_ref, res_ref, freq_ref = refs[groups:]
    total = groups * count
    facet = lax.axis_index("facet")
    x_start = facet % ACROSS * FACET - GRID // 2
    for g in range(groups):
        for s in range(count):
            d = g * count + s
            u_other = group_corner(corner_ref, near_refs, g, groups, s)
            freq_ref[d : d + 1, :] = jnp.full((1, LANES), u_other, I32)
    freq = freq_ref[...]
    low = iota((FROWS, LANES), 1) < SUB
    cos_x, sin_x = phase_pair((freq + (iota(freq.shape, 1) & (SUB - 1))) * x_start)
    sin_x = jnp.where(iota(freq.shape, 1) < SUB, -sin_x, sin_x)
    left = []
    for d in range(total):
        block = got_ref[16 * d : 16 * d + 8, :]
        moved = block * cos_x[d : d + 1] + pltpu.roll(block, SUB, 1) * sin_x[d : d + 1]
        left.append(jnp.where(low, moved, -moved))
        left.append(pltpu.roll(moved, SUB, 1))
    left = jnp.concatenate(left, axis=0).astype(BF16)
    cos_u, sin_u = phase_rows(freq)
    both = dot_nn(left, table_ref[...])
    dirty = jnp.zeros((FROWS, FACET), F32)
    for d in range(total):
        dirty = dirty + both[16 * d : 16 * d + 8] * cos_u[d : d + 1]
        dirty = dirty - both[16 * d + 8 : 16 * d + 16] * sin_u[d : d + 1]
    out_ref[...] = image_ref[...] + (GAIN_STEP * scale) * dirty

    owner_row = owner_ref[...]
    rows = owner_row.shape[1]
    hits, rank = slot_parts(owner_row, count)
    first = lax.axis_index("freq") * (count * 16)
    back = [got_ref[pl.ds(pl.multiple_of(first + 16 * s + 8, 8), 8), :] for s in range(count)]
    place = (iota((LANES, rows), 0) == rank).astype(F32)
    found = dot_nn(jnp.concatenate(back, axis=0), place, exact_products)
    picked = jnp.zeros((8, rows), F32)
    for s in range(count):
        picked = picked + found[8 * s : 8 * s + 8] * hits[s : s + 1]
    res_ref[...] = picked[0:2]


def on_device(model_image, visibilities, kernel_u, kernel_v, owners, offsets, corners):
    count = lax.axis_size("facet")
    groups = lax.axis_size("freq")
    rows = owners.shape[0]
    cap = 4 * rows // count
    assert count % ACROSS == 0 and LANES % cap == 0
    scale = 1.0 / math.sqrt(count * FROWS * FACET)
    lane_groups, row_blocks, piece = layout_of(cap)
    height = count // ACROSS * FROWS
    slots = count * cap
    total = groups * count
    corner = corners.reshape(2 * count)
    near = [
        lax.ppermute(corner, "freq", [(g, (g + k) % groups) for g in range(groups)])
        for k in range(1, groups)
    ]
    owner_row = owners.reshape(1, rows)
    smem = pl.BlockSpec(memory_space=pltpu.SMEM)
    vmem = pl.BlockSpec(memory_space=pltpu.VMEM)
    params = pltpu.CompilerParams(vmem_limit_bytes=48 * 1024 * 1024)

    def shape(*dims, dtype=F32):
        return jax.ShapeDtypeStruct(dims, dtype)

    def call(body, out_shape, scalars, arrays, name, scratch=(), **sizes):
        return pl.pallas_call(
            lambda *refs: body(*refs, **sizes),
            out_shape=out_shape,
            in_specs=[smem] * len(scalars) + [vmem] * len(arrays),
            out_specs=jax.tree.map(lambda _: vmem, out_shape),
            scratch_shapes=scratch,
            compiler_params=params,
            name=name,
        )(*scalars, *arrays)

    send, table = call(
        send_kernel,
        (shape(count * piece, LANES), shape(2 * SUB, FACET, dtype=BF16)),
        [corner],
        [owner_row, visibilities, kernel_u, kernel_v, offsets, model_image],
        "send_rows",
        [pltpu.VMEM((count, LANES), I32), pltpu.VMEM((16 * count, FACET), BF16)],
        count=count,
        cap=cap,
    )
    got = lax.all_to_all(send, "facet", split_axis=0, concat_axis=0, tiled=True)
    columns, kern_u, kern_h, vis, spread, own = call(
        first_kernel,
        (
            shape(height, LANES),
            shape(SUB, slots),
            shape(2 * height, slots),
            shape(8, slots),
            shape(total * height, LANES),
            shape(height, LANES),
        ),
        [corner],
        [got],
        "first_cycle",
        count=count,
        cap=cap,
        groups=groups,
        scale=scale,
    )
    everyone = lax.all_to_all(spread, ("freq", "facet"), split_axis=0, concat_axis=0, tiled=True)
    back = call(
        second_kernel,
        shape(total * 16, LANES),
        [corner, *near],
        [everyone, own, columns, kern_u, kern_h, vis],
        "second_cycle",
        [pltpu.VMEM((height, LANES), F32)],
        count=count,
        cap=cap,
        groups=groups,
        scale=scale,
    )
    returned = lax.all_to_all(back, ("freq", "facet"), split_axis=0, concat_axis=0, tiled=True)
    return call(
        image_kernel,
        (shape(FROWS, FACET), shape(2, rows)),
        [corner, *near],
        [returned, table, owner_row, model_image],
        "form_image",
        [pltpu.VMEM((total, LANES), I32)],
        count=count,
        groups=groups,
        scale=scale,
    )


def solution(mesh):
    return jax.shard_map(
        on_device,
        mesh=mesh,
        in_specs=(
            P("facet", None),
            P(None, ("freq", "facet")),
            P(None, ("freq", "facet")),
            P(None, ("freq", "facet")),
            P(("freq", "facet"), None),
            P(None, ("freq", "facet")),
            P("freq", None, None),
        ),
        out_specs=(P("facet", None), P(None, ("freq", "facet"))),
        check_vma=False,
    )
```

```python
import math

import jax
import jax.numpy as jnp
from jax import lax
from jax.experimental import pallas as pl
from jax.experimental.pallas import tpu as pltpu
from jax.sharding import PartitionSpec as P

GRID = 16384
FACET = 2048
FROWS = 8
SUB = 64
SUPPORT = 16
LANES = 128
ACROSS = GRID // FACET
GROUPS = 6
BACK = FROWS + 1
GAIN_STEP = 0.5

F32 = jnp.float32
BF16 = jnp.bfloat16
I32 = jnp.int32
exact_products = lax.Precision.HIGHEST


def iota(shape, dim):
    return lax.broadcasted_iota(I32, shape, dim)


def phase_pair(index):
    moved = index + GRID // 8
    quadrant = (moved >> 12) & 3
    angle = ((moved & (GRID // 4 - 1)) - GRID // 8).astype(F32) * (2.0 * math.pi / GRID)
    sq = angle * angle
    sin_p = angle * (1.0 + sq * (-1.0 / 6 + sq * (1.0 / 120 + sq * (-1.0 / 5040 + sq * (1.0 / 362880)))))
    cos_p = 1.0 + sq * (-0.5 + sq * (1.0 / 24 + sq * (-1.0 / 720 + sq * (1.0 / 40320))))
    swap = (quadrant & 1) == 1
    cos_v = jnp.where(swap, sin_p, cos_p)
    sin_v = jnp.where(swap, cos_p, sin_p)
    cos_v = jnp.where((quadrant == 1) | (quadrant == 2), -cos_v, cos_v)
    sin_v = jnp.where(quadrant >= 2, -sin_v, sin_v)
    return cos_v, sin_v


def phase_rows(freq):
    cos_v, sin_v = phase_pair(freq * iota(freq.shape, 1))
    turn_c, turn_s = phase_pair(freq * LANES)
    cos_l, sin_l = [cos_v], [sin_v]
    while len(cos_l) < FACET // LANES:
        more_c = [c * turn_c - s * turn_s for c, s in zip(cos_l, sin_l)]
        more_s = [s * turn_c + c * turn_s for c, s in zip(cos_l, sin_l)]
        cos_l, sin_l = cos_l + more_c, sin_l + more_s
        turn_c, turn_s = turn_c * turn_c - turn_s * turn_s, 2.0 * turn_c * turn_s
    return jnp.concatenate(cos_l, axis=1), jnp.concatenate(sin_l, axis=1)


def dot_nt(left, right, precision=None):
    return lax.dot_general(
        left, right, (((1,), (1,)), ((), ())), precision=precision, preferred_element_type=F32
    )


def dot_nn(left, right, precision=None):
    return lax.dot_general(
        left, right, (((1,), (0,)), ((), ())), precision=precision, preferred_element_type=F32
    )


def layout_of(cap):
    lane_groups = LANES // cap
    row_blocks = -(-GROUPS // lane_groups)
    rows = 8 * row_blocks - (6 if row_blocks == 3 else 0)
    return lane_groups, row_blocks, FROWS + rows


def read_block(ref, start, rows):
    block = ref[start : start + rows, :]
    return block if rows == 8 else jnp.concatenate([block, jnp.zeros((8 - rows, LANES), F32)], axis=0)


def slot_parts(owner_row, count):
    rows = owner_row.shape[1]
    hits = (iota((count, rows), 0) == owner_row).astype(F32)
    earlier = (iota((rows, rows), 0) < iota((rows, rows), 1)).astype(F32)
    before = dot_nn(hits.astype(BF16), earlier.astype(BF16))
    return hits, jnp.sum(before * hits, axis=0, keepdims=True).astype(I32)


def splat_rows(corner_ref, target_ref, start, count):
    for s in range(count):
        target_ref[start + s : start + s + 1, :] = jnp.full((1, LANES), corner_ref[0, s], I32)


def send_kernel(
    corner_ref, owner_hbm, vis_hbm, ku_hbm, kv_hbm, off_hbm, image_hbm,
    send_ref, table_ref, hits_ref, rank_ref,
    owner_ref, vis_ref, ku_ref, kv_ref, off_ref, image_ref, freq_ref, mod_ref, sem_ref, *, count, cap,
):
    lane_groups, row_blocks, piece = layout_of(cap)
    sources = [image_hbm, owner_hbm, vis_hbm, ku_hbm, kv_hbm, off_hbm]
    targets = [image_ref, owner_ref, vis_ref, ku_ref, kv_ref, off_ref]
    copies = [
        pltpu.make_async_copy(src, dst, sem_ref.at[i]) for i, (src, dst) in enumerate(zip(sources, targets))
    ]
    for copy in copies:
        copy.start()
    facet = lax.axis_index("facet")
    x_start = facet % ACROSS * FACET - GRID // 2
    splat_rows(corner_ref, freq_ref, 0, count)
    freq = freq_ref[...]
    cos_t, sin_t = phase_rows(iota((SUB, LANES), 0))
    table = jnp.concatenate([cos_t, sin_t], axis=0).astype(BF16)
    table_ref[...] = table
    cos_u, sin_u = phase_rows(freq)
    for copy in copies:
        copy.wait()
    image = image_ref[...]
    for s in range(count):
        both = jnp.concatenate([image * cos_u[s : s + 1], -image * sin_u[s : s + 1]], axis=0)
        mod_ref[16 * s : 16 * s + 16, :] = both.astype(BF16)
    prod = dot_nt(mod_ref[...], table)
    lane = iota((FROWS, LANES), 1)
    low = lane < SUB
    cos_x, sin_x = phase_pair((freq + (iota(freq.shape, 1) & (SUB - 1))) * x_start)
    sin_x = jnp.where(iota(freq.shape, 1) < SUB, sin_x, -sin_x)
    for s in range(count):
        real_p = prod[16 * s : 16 * s + 8]
        imag_p = pltpu.roll(prod[16 * s + 8 : 16 * s + 16], SUB, 1)
        col = jnp.where(low, real_p + imag_p, imag_p - real_p)
        send_ref[piece * s : piece * s + FROWS, :] = (
            col * cos_x[s : s + 1] + pltpu.roll(col, SUB, 1) * sin_x[s : s + 1]
        )

    owner_row = owner_ref[...]
    rows = owner_row.shape[1]
    hits, rank = slot_parts(owner_row, count)
    hits_ref[...] = hits
    rank_ref[...] = rank
    blank = jnp.zeros((6, rows), F32)
    vis = jnp.concatenate([vis_ref[...], blank], axis=0)
    offset = jnp.concatenate([off_ref[...].astype(F32), blank], axis=0)
    parts = [ku_ref[0:8, :], ku_ref[8:16, :], vis, kv_ref[0:8, :], kv_ref[8:16, :], offset]
    total = None
    for group in range(-(-GROUPS // row_blocks)):
        mine = parts[group * row_blocks : (group + 1) * row_blocks]
        stacked = jnp.concatenate(mine, axis=0)
        masked = jnp.concatenate([stacked * hits[s : s + 1] for s in range(count)], axis=0)
        place = (iota((LANES, rows), 0) == rank + group * cap).astype(F32)
        moved = dot_nt(masked, place, exact_products)
        total = moved if total is None else total + moved
    for s in range(count):
        at = 8 * row_blocks * s
        send_ref[piece * s + FROWS : piece * (s + 1), :] = total[at : at + piece - FROWS]


def place_kernel(taps, offset):
    low = jnp.concatenate([taps, jnp.zeros((8, LANES), F32)], axis=0)
    for step in (1, 2, 4):
        bit = jnp.broadcast_to((offset & step) != 0, low.shape)
        low = jnp.where(bit, pltpu.roll(low, step, 0), low)
    zero = jnp.zeros((8, LANES), F32)
    blocks = [low[0:8], low[8:16], low[16:24]]
    for step in (1, 2, 4):
        bit = jnp.broadcast_to((offset & (8 * step)) != 0, (8, LANES))
        size = min(len(blocks) + step, SUB // 8)
        wide = blocks + [zero] * (size - len(blocks))
        blocks = [jnp.where(bit, wide[k - step] if k >= step else zero, wide[k]) for k in range(size)]
    return jnp.concatenate(blocks, axis=0)


def predict(column_rows, kern_u, kern_h, vis, scale):
    height = column_rows.shape[0]
    stacked = jnp.concatenate([column_rows[:, :SUB], column_rows[:, SUB:]], axis=0)
    partial = dot_nn(stacked, kern_u, exact_products)
    part_re, part_im = partial[:height], partial[height:]
    h_re, h_im = kern_h[:height], kern_h[height:]
    pred_re = jnp.sum(h_re * part_re - h_im * part_im, axis=0, keepdims=True)
    pred_im = jnp.sum(h_re * part_im + h_im * part_re, axis=0, keepdims=True)
    return vis[0:1] - scale * pred_re, vis[1:2] - scale * pred_im


def grid_rows(res_re, res_im, kern_u, kern_h):
    height = kern_h.shape[0] // 2
    h_re, h_im = kern_h[:height], kern_h[height:]
    spread = jnp.concatenate([h_re * res_re + h_im * res_im, h_re * res_im - h_im * res_re], axis=0)
    rows = dot_nt(spread, kern_u, exact_products)
    return jnp.concatenate([rows[:height], rows[height:]], axis=1)


def first_kernel(
    corner_ref, got_ref, col_ref, ku_ref, kh_ref, vis_ref, rows_ref, own_ref, *, count, cap, groups, scale,
):
    lane_groups, row_blocks, piece = layout_of(cap)
    height = count // ACROSS * FROWS
    v_start = corner_ref[1, lax.axis_index("facet")]
    sums = []
    for down in range(count // ACROSS):
        total = got_ref[piece * down * ACROSS : piece * down * ACROSS + FROWS, :]
        for across in range(1, ACROSS):
            at = piece * (down * ACROSS + across)
            total = total + got_ref[at : at + FROWS, :]
        sums.append(total)
    columns = jnp.concatenate(sums, axis=0)
    col_ref[...] = columns
    lane_group = iota((8, LANES), 1) // cap
    u_list, v_list, vis_list = [], [], []
    for tile in range(count // lane_groups):
        found = []
        for k in range(GROUPS):
            block, group = k % row_blocks, k // row_blocks
            value = None
            for j in range(lane_groups):
                at = FROWS + 8 * block
                moved = read_block(got_ref, piece * (tile * lane_groups + j) + at, min(8, piece - at))
                shift = (j - group) * cap % LANES
                if shift:
                    moved = pltpu.roll(moved, shift, 1)
                value = moved if value is None else jnp.where(lane_group == j, moved, value)
            found.append(value)
        offset = found[5].astype(I32)
        u_list.append(place_kernel(jnp.concatenate(found[0:2], axis=0), offset[0:1]))
        v_list.append(place_kernel(jnp.concatenate(found[3:5], axis=0), offset[1:2]))
        vis_list.append(found[2])
    kern_u = jnp.concatenate(u_list, axis=1)
    kern_v = jnp.concatenate(v_list, axis=1)
    vis = jnp.concatenate(vis_list, axis=1)
    row = iota((height, SUB), 0)
    y_pos = row // FROWS * FACET - GRID // 2 + row % FROWS
    cos_y, sin_y = phase_pair((v_start + iota((height, SUB), 1)) * y_pos)
    kern_h = dot_nn(jnp.concatenate([cos_y, -sin_y], axis=0), kern_v, exact_products)
    ku_ref[...] = kern_u
    kh_ref[...] = kern_h
    vis_ref[...] = vis
    res_re, res_im = predict(columns, kern_u, kern_h, vis, scale)
    rows = grid_rows(res_re, res_im, kern_u, kern_h)
    own_ref[...] = rows
    for d in range(groups * count):
        rows_ref[height * d : height * (d + 1), :] = rows


def group_corner(corner_ref, near_refs, group, groups, index):
    refs = [corner_ref] + list(near_refs)
    back = (lax.axis_index("freq") - group) % groups
    value = refs[0][0, index]
    for k in range(1, groups):
        value = jnp.where(back == k, refs[k][0, index], value)
    return value


def turn(value, shift):
    shift = shift % LANES
    return pltpu.roll(value, shift, 1) if shift else value


def second_kernel(*refs, count, cap, groups, scale):
    corner_ref, near_refs = refs[0], refs[1:groups]
    all_ref, own_ref, col_ref, ku_ref, kh_ref, vis_ref, back_ref, sum_ref = refs[groups:]
    lane_groups = LANES // cap
    height = col_ref.shape[0]
    u_start = corner_ref[0, lax.axis_index("facet")]
    sum_ref[...] = jnp.zeros_like(sum_ref)
    row, col = iota((LANES, LANES), 0), iota((LANES, LANES), 1)
    same = (row < SUB) == (col < SUB)
    row_a, col_a = row & (SUB - 1), col & (SUB - 1)
    sign = jnp.where(col < SUB, 1.0, -1.0)
    half = GRID // 2

    def overlap(d, carry):
        u_other = group_corner(corner_ref, near_refs, d // count, groups, d % count)
        ahead = ((u_start - u_other + half) & (GRID - 1)) - half
        mirror = (-u_start - u_other) & (GRID - 1)

        @pl.when(((ahead > -SUB) & (ahead < SUB)) | (mirror < 2 * SUB - 1))
        def _():
            select = jnp.where(same & (row_a == col_a + ahead), 1.0, 0.0)
            select = select + jnp.where(same & (row_a + col_a == mirror), sign, 0.0)
            block = all_ref[pl.ds(pl.multiple_of(d * height, 8), height), :]
            sum_ref[...] += dot_nn(block, select, exact_products)

        return carry

    lax.fori_loop(0, groups * count, overlap, 0)
    columns = col_ref[...] + (GAIN_STEP * scale * (GRID / 2)) * sum_ref[...]
    kern_u, kern_h = ku_ref[...], kh_ref[...]
    res_re, res_im = predict(columns, kern_u, kern_h, vis_ref[...], scale)
    rows = own_ref[...] + grid_rows(res_re, res_im, kern_u, kern_h)
    tiles = count // lane_groups
    res_re = jnp.concatenate([res_re[:, LANES * t : LANES * (t + 1)] for t in range(tiles)], axis=0)
    res_im = jnp.concatenate([res_im[:, LANES * t : LANES * (t + 1)] for t in range(tiles)], axis=0)
    low = iota((tiles, LANES), 1) < cap
    back = [
        jnp.where(low, turn(res_re, -j * cap), turn(res_im, (1 - j) * cap)) for j in range(lane_groups)
    ]
    for s in range(count):
        tile, j, down = s // lane_groups, s % lane_groups, s // ACROSS
        for g in range(groups):
            at = BACK * (g * count + s)
            back_ref[at : at + 8, :] = rows[8 * down : 8 * down + 8]
            back_ref[at + 8 : at + 9, :] = back[j][tile : tile + 1]


def phase_kernel(*refs, count, groups):
    corner_ref, near_refs = refs[0], refs[1:groups]
    cos_ref, sin_ref, cos_x_ref, sin_x_ref, freq_ref = refs[groups:]
    x_start = lax.axis_index("facet") % ACROSS * FACET - GRID // 2
    for g in range(groups):
        for s in range(count):
            u_other = group_corner(corner_ref, near_refs, g, groups, s)
            freq_ref[g * count + s : g * count + s + 1, :] = jnp.full((1, LANES), u_other, I32)
    freq = freq_ref[...]
    cos_x, sin_x = phase_pair((freq + (iota(freq.shape, 1) & (SUB - 1))) * x_start)
    cos_x_ref[...] = cos_x
    sin_x_ref[...] = jnp.where(iota(freq.shape, 1) < SUB, -sin_x, sin_x)
    cos_ref[...], sin_ref[...] = phase_rows(freq)


def image_kernel(
    got_ref, table_ref, cos_ref, sin_ref, cos_x_ref, sin_x_ref, hits_ref, rank_ref, image_ref,
    out_ref, res_ref, *, count, groups, cap, scale,
):
    total = groups * count
    low = iota((FROWS, LANES), 1) < SUB
    cos_x, sin_x = cos_x_ref[...], sin_x_ref[...]
    left = []
    for d in range(total):
        block = got_ref[BACK * d : BACK * d + 8, :]
        moved = block * cos_x[d : d + 1] + pltpu.roll(block, SUB, 1) * sin_x[d : d + 1]
        left.append(jnp.where(low, moved, -moved))
        left.append(pltpu.roll(moved, SUB, 1))
    left = jnp.concatenate(left, axis=0).astype(BF16)
    both = dot_nn(left, table_ref[...])
    dirty = jnp.zeros((FROWS, FACET), F32)
    for d in range(total):
        dirty = dirty + both[16 * d : 16 * d + 8] * cos_ref[d : d + 1, :]
        dirty = dirty - both[16 * d + 8 : 16 * d + 16] * sin_ref[d : d + 1, :]
    out_ref[...] = image_ref[...] + (GAIN_STEP * scale) * dirty

    rows = rank_ref.shape[1]
    first = lax.axis_index("freq") * (count * BACK) + 8
    back = jnp.concatenate([got_ref[pl.ds(first + BACK * s, 1), :] for s in range(count)], axis=0)
    picked = []
    for part in range(2):
        place = (iota((LANES, rows), 0) == rank_ref[...] + part * cap).astype(F32)
        found = dot_nn(back, place, exact_products)
        picked.append(jnp.sum(found * hits_ref[...], axis=0, keepdims=True))
    res_ref[...] = jnp.concatenate(picked, axis=0)


def on_device(model_image, visibilities, kernel_u, kernel_v, owners, offsets, corners):
    count = lax.axis_size("facet")
    groups = lax.axis_size("freq")
    rows = owners.shape[0]
    cap = 4 * rows // count
    assert count % ACROSS == 0 and 2 * cap <= LANES and LANES % cap == 0
    scale = 1.0 / math.sqrt(count * FROWS * FACET)
    lane_groups, row_blocks, piece = layout_of(cap)
    height = count // ACROSS * FROWS
    slots = count * cap
    total = groups * count
    corner = corners[0].T
    near = [
        lax.ppermute(corner, "freq", [(g, (g + k) % groups) for g in range(groups)])
        for k in range(1, groups)
    ]
    owner_row = owners.reshape(1, rows)
    smem = pl.BlockSpec(memory_space=pltpu.SMEM)
    vmem = pl.BlockSpec(memory_space=pltpu.VMEM)
    far = pl.BlockSpec(memory_space=pltpu.HBM)
    params = pltpu.CompilerParams(vmem_limit_bytes=48 * 1024 * 1024)

    def shape(*dims, dtype=F32):
        return jax.ShapeDtypeStruct(dims, dtype)

    def call(body, out_shape, scalars, arrays, name, scratch=(), space=vmem, **sizes):
        return pl.pallas_call(
            lambda *refs: body(*refs, **sizes),
            out_shape=out_shape,
            in_specs=[smem] * len(scalars) + [space] * len(arrays),
            out_specs=jax.tree.map(lambda _: vmem, out_shape),
            scratch_shapes=scratch,
            compiler_params=params,
            name=name,
        )(*scalars, *arrays)

    def exchange(block, axes, parts):
        view = block.reshape(parts, 1, block.size // parts)
        return lax.all_to_all(view, axes, split_axis=0, concat_axis=0, tiled=True).reshape(block.shape)

    inputs = [owner_row, visibilities, kernel_u, kernel_v, offsets]
    send, table, hits, rank = call(
        send_kernel,
        (
            shape(count * piece, LANES),
            shape(2 * SUB, FACET, dtype=BF16),
            shape(count, rows),
            shape(1, rows, dtype=I32),
        ),
        [corner],
        [pltpu.with_memory_space_constraint(x, pltpu.HBM) for x in [*inputs, model_image]],
        "send_rows",
        [pltpu.VMEM(x.shape, x.dtype) for x in [*inputs, model_image]]
        + [
            pltpu.VMEM((count, LANES), I32),
            pltpu.VMEM((16 * count, FACET), BF16),
            pltpu.SemaphoreType.DMA((6,)),
        ],
        far,
        count=count,
        cap=cap,
    )
    got = exchange(send, "facet", count)
    columns, kern_u, kern_h, vis, spread, own = call(
        first_kernel,
        (
            shape(height, LANES),
            shape(SUB, slots),
            shape(2 * height, slots),
            shape(8, slots),
            shape(total * height, LANES),
            shape(height, LANES),
        ),
        [corner],
        [got],
        "first_cycle",
        count=count,
        cap=cap,
        groups=groups,
        scale=scale,
    )
    everyone = exchange(spread, ("freq", "facet"), total)
    phases = call(
        phase_kernel,
        (shape(total, FACET), shape(total, FACET), shape(total, LANES), shape(total, LANES)),
        [corner, *near],
        [],
        "phases",
        [pltpu.VMEM((total, LANES), I32)],
        count=count,
        groups=groups,
    )
    back = call(
        second_kernel,
        shape(total * BACK, LANES),
        [corner, *near],
        [everyone, own, columns, kern_u, kern_h, vis],
        "second_cycle",
        [pltpu.VMEM((height, LANES), F32)],
        count=count,
        cap=cap,
        groups=groups,
        scale=scale,
    )
    returned = exchange(back, ("freq", "facet"), total)
    return call(
        image_kernel,
        (shape(FROWS, FACET), shape(2, rows)),
        [],
        [returned, table, *phases, hits, rank, model_image],
        "form_image",
        count=count,
        groups=groups,
        cap=cap,
        scale=scale,
    )


def solution(mesh):
    return jax.shard_map(
        on_device,
        mesh=mesh,
        in_specs=(
            P("facet", None),
            P(None, ("freq", "facet")),
            P(None, ("freq", "facet")),
            P(None, ("freq", "facet")),
            P(("freq", "facet"), None),
            P(None, ("freq", "facet")),
            P("freq", None, None),
        ),
        out_specs=(P("facet", None), P(None, ("freq", "facet"))),
        check_vma=False,
    )
```

```python
import math

import jax
import jax.numpy as jnp
from jax import lax
from jax.experimental import pallas as pl
from jax.experimental.pallas import tpu as pltpu
from jax.sharding import PartitionSpec as P

GRID = 16384
FACET = 2048
FROWS = 8
SUB = 64
SUPPORT = 16
LANES = 128
ACROSS = GRID // FACET
GROUPS = 6
BACK = FROWS + 1
GAIN_STEP = 0.5

F32 = jnp.float32
BF16 = jnp.bfloat16
I32 = jnp.int32
exact_products = lax.Precision.HIGHEST


def iota(shape, dim):
    return lax.broadcasted_iota(I32, shape, dim)


def phase_pair(index):
    moved = index + GRID // 8
    quadrant = (moved >> 12) & 3
    angle = ((moved & (GRID // 4 - 1)) - GRID // 8).astype(F32) * (2.0 * math.pi / GRID)
    sq = angle * angle
    sin_p = angle * (1.0 + sq * (-1.0 / 6 + sq * (1.0 / 120 + sq * (-1.0 / 5040 + sq * (1.0 / 362880)))))
    cos_p = 1.0 + sq * (-0.5 + sq * (1.0 / 24 + sq * (-1.0 / 720 + sq * (1.0 / 40320))))
    swap = (quadrant & 1) == 1
    cos_v = jnp.where(swap, sin_p, cos_p)
    sin_v = jnp.where(swap, cos_p, sin_p)
    cos_v = jnp.where((quadrant == 1) | (quadrant == 2), -cos_v, cos_v)
    sin_v = jnp.where(quadrant >= 2, -sin_v, sin_v)
    return cos_v, sin_v


def phase_rows(freq):
    cos_v, sin_v = phase_pair(freq * iota(freq.shape, 1))
    turn_c, turn_s = phase_pair(freq * LANES)
    cos_l, sin_l = [cos_v], [sin_v]
    while len(cos_l) < FACET // LANES:
        more_c = [c * turn_c - s * turn_s for c, s in zip(cos_l, sin_l)]
        more_s = [s * turn_c + c * turn_s for c, s in zip(cos_l, sin_l)]
        cos_l, sin_l = cos_l + more_c, sin_l + more_s
        turn_c, turn_s = turn_c * turn_c - turn_s * turn_s, 2.0 * turn_c * turn_s
    return jnp.concatenate(cos_l, axis=1), jnp.concatenate(sin_l, axis=1)


def dot_nt(left, right, precision=None):
    return lax.dot_general(
        left, right, (((1,), (1,)), ((), ())), precision=precision, preferred_element_type=F32
    )


def dot_nn(left, right, precision=None):
    return lax.dot_general(
        left, right, (((1,), (0,)), ((), ())), precision=precision, preferred_element_type=F32
    )


def split(value):
    high = value.astype(BF16)
    return jnp.concatenate([high, (value - high.astype(F32)).astype(BF16)], axis=0)


def fold(value):
    half = value.shape[0] // 2
    return value[:half] + value[half:]


def spread_row(ref, row):
    return ref[pl.ds(row, FROWS, stride=0), :]


def layout_of(cap):
    lane_groups = LANES // cap
    row_blocks = -(-GROUPS // lane_groups)
    rows = 8 * row_blocks - (6 if row_blocks == 3 else 0)
    return lane_groups, row_blocks, FROWS + rows


def read_block(ref, start, rows):
    block = ref[start : start + rows, :]
    return block if rows == 8 else jnp.concatenate([block, jnp.zeros((8 - rows, LANES), F32)], axis=0)


def slot_parts(owner_row, count):
    rows = owner_row.shape[1]
    hits = (iota((count, rows), 0) == owner_row).astype(F32)
    earlier = (iota((rows, rows), 0) < iota((rows, rows), 1)).astype(F32)
    before = dot_nn(hits.astype(BF16), earlier.astype(BF16))
    return hits, jnp.sum(before * hits, axis=0, keepdims=True).astype(I32)


def send_kernel(
    corner_hbm, owner_hbm, vis_hbm, ku_hbm, kv_hbm, off_hbm, image_hbm,
    send_ref, table_ref, hits_ref, rank_ref, corner_out,
    corner_ref, owner_ref, vis_ref, ku_ref, kv_ref, off_ref, image_ref,
    freq_ref, cos_ref, sin_ref, mod_ref, sem_ref, *, count, cap,
):
    lane_groups, row_blocks, piece = layout_of(cap)
    sources = [corner_hbm, image_hbm, owner_hbm, vis_hbm, ku_hbm, kv_hbm, off_hbm, corner_hbm]
    targets = [corner_ref, image_ref, owner_ref, vis_ref, ku_ref, kv_ref, off_ref, corner_out]
    copies = [
        pltpu.make_async_copy(src, dst, sem_ref.at[i]) for i, (src, dst) in enumerate(zip(sources, targets))
    ]
    for copy in copies:
        copy.start()
    facet = lax.axis_index("facet")
    x_start = facet % ACROSS * FACET - GRID // 2
    cos_t, sin_t = phase_rows(iota((SUB, LANES), 0))
    table = jnp.concatenate([cos_t, sin_t], axis=0).astype(BF16)
    table_ref[...] = table
    copies[0].wait()
    for s in range(count):
        freq_ref[s : s + 1, :] = jnp.full((1, LANES), corner_ref[0, s], I32)
    freq = freq_ref[...]
    cos_ref[...], sin_ref[...] = phase_rows(freq)
    for copy in copies[1:]:
        copy.wait()
    image = image_ref[...]
    for s in range(count):
        both = jnp.concatenate([image * spread_row(cos_ref, s), -image * spread_row(sin_ref, s)], axis=0)
        mod_ref[16 * s : 16 * s + 16, :] = both.astype(BF16)
    prod = dot_nt(mod_ref[...], table)
    lane = iota((FROWS, LANES), 1)
    low = lane < SUB
    cos_x, sin_x = phase_pair((freq + (iota(freq.shape, 1) & (SUB - 1))) * x_start)
    sin_x = jnp.where(iota(freq.shape, 1) < SUB, sin_x, -sin_x)
    for s in range(count):
        real_p = prod[16 * s : 16 * s + 8]
        imag_p = pltpu.roll(prod[16 * s + 8 : 16 * s + 16], SUB, 1)
        col = jnp.where(low, real_p + imag_p, imag_p - real_p)
        send_ref[piece * s : piece * s + FROWS, :] = (
            col * cos_x[s : s + 1] + pltpu.roll(col, SUB, 1) * sin_x[s : s + 1]
        )

    owner_row = owner_ref[...]
    rows = owner_row.shape[1]
    hits, rank = slot_parts(owner_row, count)
    hits_ref[...] = hits
    rank_ref[...] = rank
    blank = jnp.zeros((6, rows), F32)
    vis = jnp.concatenate([vis_ref[...], blank], axis=0)
    offset = jnp.concatenate([off_ref[...].astype(F32), blank], axis=0)
    parts = [ku_ref[0:8, :], ku_ref[8:16, :], vis, kv_ref[0:8, :], kv_ref[8:16, :], offset]
    parts = parts + [jnp.zeros((8, rows), F32)] * (-len(parts) % row_blocks)
    groups = len(parts) // row_blocks
    high = 16 * -(-row_blocks // 2)
    left, places = [], []
    for group in range(groups):
        mine = parts[group * row_blocks : (group + 1) * row_blocks]
        mine = mine + [jnp.zeros((8, rows), F32)] * (high // 8 - row_blocks)
        both = split(jnp.concatenate(mine, axis=0))
        place = (iota((LANES, rows), 0) == rank + group * cap).astype(F32).astype(BF16)
        left += [both[:high], both[high:]]
        places += [place, place]
    stacked = jnp.concatenate(left, axis=1)
    wide = jnp.concatenate([hits] * (2 * groups), axis=1)
    masked = [
        stacked * jnp.broadcast_to(wide[s : s + 1], stacked.shape).astype(BF16) for s in range(count)
    ]
    total = dot_nt(jnp.concatenate(masked, axis=0), jnp.concatenate(places, axis=1))
    for s in range(count):
        send_ref[piece * s + FROWS : piece * (s + 1), :] = total[high * s : high * s + piece - FROWS]


def place_kernel(taps, offset):
    low = jnp.concatenate([taps, jnp.zeros((8, LANES), F32)], axis=0)
    for step in (1, 2, 4):
        bit = jnp.broadcast_to((offset & step) != 0, low.shape)
        low = jnp.where(bit, pltpu.roll(low, step, 0), low)
    zero = jnp.zeros((8, LANES), F32)
    blocks = [low[0:8], low[8:16], low[16:24]]
    for step in (1, 2, 4):
        bit = jnp.broadcast_to((offset & (8 * step)) != 0, (8, LANES))
        size = min(len(blocks) + step, SUB // 8)
        wide = blocks + [zero] * (size - len(blocks))
        blocks = [jnp.where(bit, wide[k - step] if k >= step else zero, wide[k]) for k in range(size)]
    return jnp.concatenate(blocks, axis=0)


def predict(columns, kern_u, kern_h, vis, scale):
    height = columns.shape[0]
    low = iota(columns.shape, 1) < SUB
    turned = pltpu.roll(columns, SUB, 1)
    twice = jnp.concatenate([jnp.where(low, columns, turned), jnp.where(low, turned, columns)], axis=0)
    partial = fold(dot_nn(split(twice), kern_u))
    part_re, part_im = partial[:height], partial[height:]
    h_re, h_im = kern_h[:height], kern_h[height:]
    pred_re = jnp.sum(h_re * part_re - h_im * part_im, axis=0, keepdims=True)
    pred_im = jnp.sum(h_re * part_im + h_im * part_re, axis=0, keepdims=True)
    return vis[0:1] - scale * pred_re, vis[1:2] - scale * pred_im


def grid_rows(res_re, res_im, kern_u, kern_h):
    height = kern_h.shape[0] // 2
    h_re, h_im = kern_h[:height], kern_h[height:]
    weighted = jnp.concatenate([h_re * res_re + h_im * res_im, h_re * res_im - h_im * res_re], axis=0)
    rows = fold(dot_nt(split(weighted), kern_u))
    rows = rows + pltpu.roll(rows, SUB, 1)
    return jnp.where(iota((height, LANES), 1) < SUB, rows[:height], rows[height:])


def first_kernel(
    corner_ref, got_ref, col_ref, ku_ref, kh_ref, vis_ref, rows_ref, own_ref, *, count, cap, groups, scale,
):
    lane_groups, row_blocks, piece = layout_of(cap)
    height = count // ACROSS * FROWS
    v_start = corner_ref[1, lax.axis_index("facet")]
    sums = []
    for down in range(count // ACROSS):
        total = got_ref[piece * down * ACROSS : piece * down * ACROSS + FROWS, :]
        for across in range(1, ACROSS):
            at = piece * (down * ACROSS + across)
            total = total + got_ref[at : at + FROWS, :]
        sums.append(total)
    columns = jnp.concatenate(sums, axis=0)
    col_ref[...] = columns
    lane_group = iota((8, LANES), 1) // cap
    u_list, v_list, vis_list = [], [], []
    for tile in range(count // lane_groups):
        found = []
        for k in range(GROUPS):
            block, group = k % row_blocks, k // row_blocks
            value = None
            for j in range(lane_groups):
                at = FROWS + 8 * block
                moved = read_block(got_ref, piece * (tile * lane_groups + j) + at, min(8, piece - at))
                shift = (j - group) * cap % LANES
                if shift:
                    moved = pltpu.roll(moved, shift, 1)
                value = moved if value is None else jnp.where(lane_group == j, moved, value)
            found.append(value)
        offset = found[5].astype(I32)
        u_list.append(place_kernel(jnp.concatenate(found[0:2], axis=0), offset[0:1]))
        v_list.append(place_kernel(jnp.concatenate(found[3:5], axis=0), offset[1:2]))
        vis_list.append(found[2])
    kern_u = jnp.concatenate(u_list, axis=1)
    kern_v = jnp.concatenate(v_list, axis=1)
    vis = jnp.concatenate(vis_list, axis=1)
    row = iota((height, LANES), 0)
    y_pos = row // FROWS * FACET - GRID // 2 + row % FROWS
    cos_y, sin_y = phase_pair((v_start + (iota((height, LANES), 1) & (SUB - 1))) * y_pos)
    kern_h = fold(dot_nn(split(jnp.concatenate([cos_y, -sin_y], axis=0)), split(kern_v)))
    kern_u = split(kern_u)
    ku_ref[...] = kern_u
    kh_ref[...] = kern_h
    vis_ref[...] = vis
    res_re, res_im = predict(columns, kern_u, kern_h, vis, scale)
    rows = grid_rows(res_re, res_im, kern_u, kern_h)
    own_ref[...] = rows
    for d in range(groups * count):
        rows_ref[height * d : height * (d + 1), :] = rows


def group_corner(corner_ref, near_refs, group, groups, index):
    refs = [corner_ref] + list(near_refs)
    back = (lax.axis_index("freq") - group) % groups
    value = refs[0][0, index]
    for k in range(1, groups):
        value = jnp.where(back == k, refs[k][0, index], value)
    return value


def turn(value, shift):
    shift = shift % LANES
    return pltpu.roll(value, shift, 1) if shift else value


def second_kernel(
    all_ref, select_ref, own_ref, col_ref, ku_ref, kh_ref, vis_ref, back_ref, *, count, cap, groups, scale,
):
    lane_groups = LANES // cap
    height = col_ref.shape[0]
    total = groups * count
    chunk = math.gcd(total, 32)

    def overlap(part, carry):
        blocks = []
        for d in range(chunk):
            at = pl.multiple_of((part * chunk + d) * height, 8)
            blocks.append(split(all_ref[pl.ds(at, height), :]))
        at = pl.multiple_of(part * chunk * LANES, LANES)
        return carry + dot_nn(jnp.concatenate(blocks, axis=1), select_ref[pl.ds(at, chunk * LANES), :])

    extra = jnp.zeros((2 * height, LANES), F32)
    if total == chunk:
        extra = overlap(0, extra)
    else:
        extra = lax.fori_loop(0, total // chunk, overlap, extra)
    columns = col_ref[...] + (GAIN_STEP * scale * (GRID / 2)) * fold(extra)
    kern_u, kern_h = ku_ref[...], kh_ref[...]
    res_re, res_im = predict(columns, kern_u, kern_h, vis_ref[...], scale)
    rows = own_ref[...] + grid_rows(res_re, res_im, kern_u, kern_h)
    tiles = count // lane_groups
    res_re = jnp.concatenate([res_re[:, LANES * t : LANES * (t + 1)] for t in range(tiles)], axis=0)
    res_im = jnp.concatenate([res_im[:, LANES * t : LANES * (t + 1)] for t in range(tiles)], axis=0)
    low = iota((tiles, LANES), 1) < cap
    back = [
        jnp.where(low, turn(res_re, -j * cap), turn(res_im, (1 - j) * cap)) for j in range(lane_groups)
    ]
    for s in range(count):
        tile, j, down = s // lane_groups, s % lane_groups, s // ACROSS
        for g in range(groups):
            at = BACK * (g * count + s)
            back_ref[at : at + 8, :] = rows[8 * down : 8 * down + 8]
            back_ref[at + 8 : at + 9, :] = back[j][tile : tile + 1]


def prepare_kernel(*refs, count, groups):
    corner_ref, near_refs = refs[0], refs[1:groups]
    cos_ref, sin_ref, cos_x_ref, sin_x_ref, select_ref, freq_ref = refs[groups:]
    facet = lax.axis_index("facet")
    x_start = facet % ACROSS * FACET - GRID // 2
    u_start = corner_ref[0, facet]
    row, col = iota((LANES, LANES), 0), iota((LANES, LANES), 1)
    same = (row < SUB) == (col < SUB)
    row_a, col_a = row & (SUB - 1), col & (SUB - 1)
    behind = jnp.where(same, row_a - col_a, GRID)
    across = jnp.where(same, row_a + col_a, GRID)
    sign = jnp.where(col < SUB, 1.0, -1.0)
    half = GRID // 2

    def fill(d, carry):
        u_other = group_corner(corner_ref, near_refs, d // count, groups, d % count)
        freq_ref[pl.ds(d, 1), :] = jnp.full((1, LANES), u_other, I32)
        ahead = ((u_start - u_other + half) & (GRID - 1)) - half
        mirror = (-u_start - u_other) & (GRID - 1)
        select = jnp.where(behind == ahead, 1.0, 0.0) + jnp.where(across == mirror, sign, 0.0)
        select_ref[pl.ds(pl.multiple_of(d * LANES, LANES), LANES), :] = select.astype(BF16)
        return carry

    lax.fori_loop(0, groups * count, fill, 0)
    freq = freq_ref[...]
    cos_x, sin_x = phase_pair((freq + (iota(freq.shape, 1) & (SUB - 1))) * x_start)
    cos_x_ref[...] = cos_x
    sin_x_ref[...] = jnp.where(iota(freq.shape, 1) < SUB, -sin_x, sin_x)
    cos_ref[...], sin_ref[...] = phase_rows(freq)


def image_kernel(
    got_ref, table_ref, cos_ref, sin_ref, cos_x_ref, sin_x_ref, hits_ref, rank_ref, image_ref,
    out_ref, res_ref, *, count, groups, cap, scale,
):
    total = groups * count
    low = iota((FROWS, LANES), 1) < SUB
    cos_x, sin_x = cos_x_ref[...], sin_x_ref[...]
    left = []
    for d in range(total):
        block = got_ref[BACK * d : BACK * d + 8, :]
        moved = block * cos_x[d : d + 1] + pltpu.roll(block, SUB, 1) * sin_x[d : d + 1]
        left.append(jnp.where(low, moved, -moved))
        left.append(pltpu.roll(moved, SUB, 1))
    left = jnp.concatenate(left, axis=0).astype(BF16)
    both = dot_nn(left, table_ref[...])
    dirty = jnp.zeros((FROWS, FACET), F32)
    for d in range(total):
        dirty = dirty + both[16 * d : 16 * d + 8] * spread_row(cos_ref, d)
        dirty = dirty - both[16 * d + 8 : 16 * d + 16] * spread_row(sin_ref, d)
    out_ref[...] = image_ref[...] + (GAIN_STEP * scale) * dirty

    rows = rank_ref.shape[1]
    first = lax.axis_index("freq") * (count * BACK) + 8
    back = jnp.concatenate([got_ref[pl.ds(first + BACK * s, 1), :] for s in range(count)], axis=0)
    picked = []
    for part in range(2):
        place = (iota((LANES, rows), 0) == rank_ref[...] + part * cap).astype(F32)
        found = dot_nn(back, place, exact_products)
        picked.append(jnp.sum(found * hits_ref[...], axis=0, keepdims=True))
    res_ref[...] = jnp.concatenate(picked, axis=0)


def on_device(model_image, visibilities, kernel_u, kernel_v, owners, offsets, corners):
    count = lax.axis_size("facet")
    groups = lax.axis_size("freq")
    rows = owners.shape[0]
    cap = 4 * rows // count
    assert count % ACROSS == 0 and 2 * cap <= LANES and LANES % cap == 0
    scale = 1.0 / math.sqrt(count * FROWS * FACET)
    lane_groups, row_blocks, piece = layout_of(cap)
    height = count // ACROSS * FROWS
    slots = count * cap
    total = groups * count
    corner = corners[0].T
    owner_row = owners.reshape(1, rows)
    smem = pl.BlockSpec(memory_space=pltpu.SMEM)
    vmem = pl.BlockSpec(memory_space=pltpu.VMEM)
    far = pl.BlockSpec(memory_space=pltpu.HBM)
    params = pltpu.CompilerParams(vmem_limit_bytes=48 * 1024 * 1024)

    def shape(*dims, dtype=F32):
        return jax.ShapeDtypeStruct(dims, dtype)

    def call(body, out_shape, scalars, arrays, name, scratch=(), space=vmem, **sizes):
        return pl.pallas_call(
            lambda *refs: body(*refs, **sizes),
            out_shape=out_shape,
            in_specs=[smem] * len(scalars) + [space] * len(arrays),
            out_specs=jax.tree.map(lambda _: vmem, out_shape),
            scratch_shapes=scratch,
            compiler_params=params,
            name=name,
        )(*scalars, *arrays)

    def exchange(block, axes, parts):
        view = block.reshape(parts, 1, block.size // parts)
        return lax.all_to_all(view, axes, split_axis=0, concat_axis=0, tiled=True).reshape(block.shape)

    inputs = [corner, owner_row, visibilities, kernel_u, kernel_v, offsets, model_image]
    send, table, hits, rank, corner = call(
        send_kernel,
        (
            shape(count * piece, LANES),
            shape(2 * SUB, FACET, dtype=BF16),
            shape(count, rows),
            shape(1, rows, dtype=I32),
            shape(*corner.shape, dtype=I32),
        ),
        [],
        [pltpu.with_memory_space_constraint(x, pltpu.HBM) for x in inputs],
        "send_rows",
        [pltpu.SMEM(corner.shape, I32)]
        + [pltpu.VMEM(x.shape, x.dtype) for x in inputs[1:]]
        + [
            pltpu.VMEM((count, LANES), I32),
            pltpu.VMEM((count, FACET), F32),
            pltpu.VMEM((count, FACET), F32),
            pltpu.VMEM((16 * count, FACET), BF16),
            pltpu.SemaphoreType.DMA((8,)),
        ],
        far,
        count=count,
        cap=cap,
    )
    near = [
        lax.ppermute(corner, "freq", [(g, (g + k) % groups) for g in range(groups)])
        for k in range(1, groups)
    ]
    got = exchange(send, "facet", count)
    columns, kern_u, kern_h, vis, spread, own = call(
        first_kernel,
        (
            shape(height, LANES),
            shape(2 * SUB, slots, dtype=BF16),
            shape(2 * height, slots),
            shape(8, slots),
            shape(total * height, LANES),
            shape(height, LANES),
        ),
        [corner],
        [got],
        "first_cycle",
        count=count,
        cap=cap,
        groups=groups,
        scale=scale,
    )
    everyone = exchange(spread, ("freq", "facet"), total)
    *phases, select = call(
        prepare_kernel,
        (
            shape(total, FACET),
            shape(total, FACET),
            shape(total, LANES),
            shape(total, LANES),
            shape(total * LANES, LANES, dtype=BF16),
        ),
        [corner, *near],
        [],
        "prepare",
        [pltpu.VMEM((total, LANES), I32)],
        count=count,
        groups=groups,
    )
    back = call(
        second_kernel,
        shape(total * BACK, LANES),
        [],
        [everyone, select, own, columns, kern_u, kern_h, vis],
        "second_cycle",
        count=count,
        cap=cap,
        groups=groups,
        scale=scale,
    )
    returned = exchange(back, ("freq", "facet"), total)
    return call(
        image_kernel,
        (shape(FROWS, FACET), shape(2, rows)),
        [],
        [returned, table, *phases, hits, rank, model_image],
        "form_image",
        count=count,
        groups=groups,
        cap=cap,
        scale=scale,
    )


def solution(mesh):
    return jax.shard_map(
        on_device,
        mesh=mesh,
        in_specs=(
            P("facet", None),
            P(None, ("freq", "facet")),
            P(None, ("freq", "facet")),
            P(None, ("freq", "facet")),
            P(("freq", "facet"), None),
            P(None, ("freq", "facet")),
            P("freq", None, None),
        ),
        out_specs=(P("facet", None), P(None, ("freq", "facet"))),
        check_vma=False,
    )
```

```python
import math

import jax
import jax.numpy as jnp
from jax import lax
from jax.experimental import pallas as pl
from jax.experimental.pallas import tpu as pltpu
from jax.sharding import PartitionSpec as P

GRID = 16384
FACET = 2048
FROWS = 8
SUB = 64
SUPPORT = 16
LANES = 128
ACROSS = GRID // FACET
GROUPS = 4
BACK = FROWS + 1
CHUNK = 512
GAIN_STEP = 0.5

F32 = jnp.float32
BF16 = jnp.bfloat16
I32 = jnp.int32
exact_products = lax.Precision.HIGHEST


def iota(shape, dim):
    return lax.broadcasted_iota(I32, shape, dim)


def phase_pair(index):
    moved = index + GRID // 8
    quadrant = (moved >> 12) & 3
    angle = ((moved & (GRID // 4 - 1)) - GRID // 8).astype(F32) * (2.0 * math.pi / GRID)
    sq = angle * angle
    sin_p = angle * (1.0 + sq * (-1.0 / 6 + sq * (1.0 / 120 + sq * (-1.0 / 5040 + sq * (1.0 / 362880)))))
    cos_p = 1.0 + sq * (-0.5 + sq * (1.0 / 24 + sq * (-1.0 / 720 + sq * (1.0 / 40320))))
    swap = (quadrant & 1) == 1
    cos_v = jnp.where(swap, sin_p, cos_p)
    sin_v = jnp.where(swap, cos_p, sin_p)
    cos_v = jnp.where((quadrant == 1) | (quadrant == 2), -cos_v, cos_v)
    sin_v = jnp.where(quadrant >= 2, -sin_v, sin_v)
    return cos_v, sin_v


def phase_tiles(freq):
    cos_v, sin_v = phase_pair(freq * iota(freq.shape, 1))
    turn_c, turn_s = phase_pair(freq * LANES)
    for tile in range(FACET // LANES):
        yield tile * LANES, cos_v, sin_v
        cos_v, sin_v = cos_v * turn_c - sin_v * turn_s, sin_v * turn_c + cos_v * turn_s


def dot_nt(left, right, precision=None):
    return lax.dot_general(
        left, right, (((1,), (1,)), ((), ())), precision=precision, preferred_element_type=F32
    )


def dot_nn(left, right, precision=None):
    return lax.dot_general(
        left, right, (((1,), (0,)), ((), ())), precision=precision, preferred_element_type=F32
    )


def split(value):
    high = value.astype(BF16)
    return jnp.concatenate([high, (value - high.astype(F32)).astype(BF16)], axis=0)


def fold(value):
    half = value.shape[0] // 2
    return value[:half] + value[half:]


def spread_row(ref, row):
    return ref[pl.ds(row, FROWS, stride=0), :]


def layout_of(cap):
    lane_groups = LANES // cap
    row_blocks = -(-GROUPS // min(lane_groups, GROUPS))
    return lane_groups, row_blocks, FROWS + 8 * row_blocks + 2


def turn(value, shift):
    shift = shift % LANES
    return pltpu.roll(value, shift, 1) if shift else value


def slot_parts(owner_row, count):
    rows = owner_row.shape[1]
    hits = (iota((count, rows), 0) == owner_row).astype(F32)
    earlier = (iota((rows, rows), 0) < iota((rows, rows), 1)).astype(F32)
    before = dot_nn(hits.astype(BF16), earlier.astype(BF16))
    return hits, jnp.sum(before * hits, axis=0, keepdims=True).astype(I32)


def send_kernel(
    corner_hbm, owner_hbm, vis_hbm, ku_hbm, kv_hbm, off_hbm, image_hbm,
    send_ref, table_ref, hits_ref, rank_ref, corner_out, start_ref,
    corner_ref, owner_ref, vis_ref, ku_ref, kv_ref, off_ref, image_ref,
    freq_ref, cos_ref, sin_ref, mod_ref, sem_ref, *, count, cap,
):
    lane_groups, row_blocks, piece = layout_of(cap)
    sources = [corner_hbm, image_hbm, owner_hbm, vis_hbm, ku_hbm, kv_hbm, off_hbm, corner_hbm]
    targets = [corner_ref, image_ref, owner_ref, vis_ref, ku_ref, kv_ref, off_ref, corner_out]
    copies = [
        pltpu.make_async_copy(src, dst, sem_ref.at[i]) for i, (src, dst) in enumerate(zip(sources, targets))
    ]
    for copy in copies:
        copy.start()
    facet = lax.axis_index("facet")
    x_start = facet % ACROSS * FACET - GRID // 2
    for at, cos_t, sin_t in phase_tiles(iota((SUB, LANES), 0)):
        table_ref[:SUB, at : at + LANES] = cos_t.astype(BF16)
        table_ref[SUB:, at : at + LANES] = sin_t.astype(BF16)
    copies[0].wait()
    start_ref[...] = jnp.full(start_ref.shape, corner_ref[1, facet], I32)
    for s in range(count):
        freq_ref[s : s + 1, :] = jnp.full((1, LANES), corner_ref[0, s], I32)
    freq = freq_ref[...]
    for at, cos_u, sin_u in phase_tiles(freq):
        cos_ref[:, at : at + LANES] = cos_u
        sin_ref[:, at : at + LANES] = -sin_u
    for copy in copies[1:]:
        copy.wait()
    image = image_ref[...]
    for s in range(count):
        both = jnp.concatenate([image * spread_row(cos_ref, s), image * spread_row(sin_ref, s)], axis=0)
        mod_ref[16 * s : 16 * s + 16, :] = both.astype(BF16)
    prod = dot_nt(mod_ref[...], table_ref[...])
    lane = iota((FROWS, LANES), 1)
    low = lane < SUB
    cos_x, sin_x = phase_pair((freq + (iota(freq.shape, 1) & (SUB - 1))) * x_start)
    sin_x = jnp.where(iota(freq.shape, 1) < SUB, sin_x, -sin_x)
    for s in range(count):
        real_p = prod[16 * s : 16 * s + 8]
        imag_p = pltpu.roll(prod[16 * s + 8 : 16 * s + 16], SUB, 1)
        col = jnp.where(low, real_p + imag_p, imag_p - real_p)
        send_ref[piece * s : piece * s + FROWS, :] = (
            col * cos_x[s : s + 1] + pltpu.roll(col, SUB, 1) * sin_x[s : s + 1]
        )

    owner_row = owner_ref[...]
    rows = owner_row.shape[1]
    hits, rank = slot_parts(owner_row, count)
    hits_ref[...] = hits
    rank_ref[...] = rank
    place = [
        (iota((LANES, rows), 0) == rank + group * cap).astype(F32).astype(BF16)
        for group in range(max(2, GROUPS // row_blocks))
    ]
    high = 16 * -(-row_blocks // 2)
    taps = jnp.concatenate([ku_ref[...], kv_ref[...]], axis=0)
    left, places = [], []
    for group in range(GROUPS // row_blocks):
        mine = taps[8 * row_blocks * group : 8 * row_blocks * (group + 1)]
        if high > 8 * row_blocks:
            mine = jnp.concatenate([mine, jnp.zeros((high - 8 * row_blocks, rows), F32)], axis=0)
        both = split(mine)
        left += [both[:high], both[high:]]
        places += [place[group], place[group]]
    stacked = jnp.concatenate(left, axis=1)
    half_hits = jnp.concatenate([hits] * len(left), axis=1)
    masked = [
        stacked * jnp.broadcast_to(half_hits[s : s + 1], stacked.shape).astype(BF16) for s in range(count)
    ]
    total = dot_nt(jnp.concatenate(masked, axis=0), jnp.concatenate(places, axis=1))
    vis, offset = vis_ref[...], off_ref[...].astype(F32)
    vis = split(jnp.concatenate([hits * vis[0:1], hits * vis[1:2]], axis=0))
    offset = jnp.concatenate([hits * offset[0:1], hits * offset[1:2]], axis=0).astype(BF16)
    misc = jnp.concatenate([vis[: 2 * count], vis[2 * count :], offset], axis=1)
    misc = dot_nt(misc, jnp.concatenate([place[0], place[0], place[1]], axis=1))
    for s in range(count):
        at = piece * (s + 1) - 2
        send_ref[piece * s + FROWS : at, :] = total[high * s : high * s + 8 * row_blocks]
        send_ref[at : at + 1, :] = misc[s : s + 1]
        send_ref[at + 1 : at + 2, :] = misc[count + s : count + s + 1]


def place_kernel(taps, offset):
    low = jnp.concatenate([taps, jnp.zeros((8, LANES), F32)], axis=0)
    for step in (1, 2, 4):
        bit = jnp.broadcast_to((offset & step) != 0, low.shape)
        low = jnp.where(bit, pltpu.roll(low, step, 0), low)
    zero = jnp.zeros((8, LANES), F32)
    blocks = [low[0:8], low[8:16], low[16:24]]
    for step in (1, 2, 4):
        bit = jnp.broadcast_to((offset & (8 * step)) != 0, (8, LANES))
        size = min(len(blocks) + step, SUB // 8)
        wide = blocks + [zero] * (size - len(blocks))
        blocks = [jnp.where(bit, wide[k - step] if k >= step else zero, wide[k]) for k in range(size)]
    return jnp.concatenate(blocks, axis=0)


def predict(columns, kern_u, kern_h, vis, scale):
    height = columns.shape[0]
    low = iota(columns.shape, 1) < SUB
    turned = pltpu.roll(columns, SUB, 1)
    twice = jnp.concatenate([jnp.where(low, columns, turned), jnp.where(low, turned, columns)], axis=0)
    partial = fold(dot_nn(split(twice), kern_u))
    part_re, part_im = partial[:height], partial[height:]
    h_re, h_im = kern_h[:height], kern_h[height:]
    pred_re = jnp.sum(h_re * part_re - h_im * part_im, axis=0, keepdims=True)
    pred_im = jnp.sum(h_re * part_im + h_im * part_re, axis=0, keepdims=True)
    return vis[0:1] - scale * pred_re, vis[1:2] - scale * pred_im


def grid_rows(res_re, res_im, kern_u, kern_h):
    height = kern_h.shape[0] // 2
    h_re, h_im = kern_h[:height], kern_h[height:]
    weighted = jnp.concatenate([h_re * res_re + h_im * res_im, h_re * res_im - h_im * res_re], axis=0)
    rows = fold(dot_nt(split(weighted), kern_u))
    rows = rows + pltpu.roll(rows, SUB, 1)
    return jnp.where(iota((height, LANES), 1) < SUB, rows[:height], rows[height:])


def first_kernel(
    start_ref, got_ref, col_ref, ku_ref, kh_ref, vis_ref, rows_ref, own_ref, *, count, cap, groups, scale,
):
    lane_groups, row_blocks, piece = layout_of(cap)
    height = count // ACROSS * FROWS
    sums = []
    for down in range(count // ACROSS):
        total = got_ref[piece * down * ACROSS : piece * down * ACROSS + FROWS, :]
        for across in range(1, ACROSS):
            at = piece * (down * ACROSS + across)
            total = total + got_ref[at : at + FROWS, :]
        sums.append(total)
    columns = jnp.concatenate(sums, axis=0)
    col_ref[...] = columns
    lane_group = iota((8, LANES), 1) // cap
    u_list, v_list, vis_list = [], [], []
    for tile in range(count // lane_groups):
        found = [None] * (GROUPS + 2)
        for j in range(lane_groups):
            base = piece * (tile * lane_groups + j)
            moved = []
            for k in range(GROUPS):
                at = base + FROWS + 8 * (k % row_blocks)
                moved.append(turn(got_ref[at : at + 8, :], (j - k // row_blocks) * cap))
            misc = got_ref[base + piece - 2 : base + piece, :]
            moved += [turn(misc, j * cap), turn(misc, (j - 1) * cap)]
            for k, value in enumerate(moved):
                mine = lane_group[: value.shape[0]] == j
                found[k] = value if j == 0 else jnp.where(mine, value, found[k])
        offset = found[5].astype(I32)
        u_list.append(place_kernel(jnp.concatenate(found[0:2], axis=0), offset[0:1]))
        v_list.append(place_kernel(jnp.concatenate(found[2:4], axis=0), offset[1:2]))
        vis_list.append(found[4])
    kern_u = jnp.concatenate(u_list, axis=1)
    kern_v = jnp.concatenate(v_list, axis=1)
    vis = jnp.concatenate(vis_list, axis=1)
    row = iota((height, LANES), 0)
    y_pos = row // FROWS * FACET - GRID // 2 + row % FROWS
    cos_y, sin_y = phase_pair((start_ref[0:1, :] + (iota((height, LANES), 1) & (SUB - 1))) * y_pos)
    kern_h = fold(dot_nn(split(jnp.concatenate([cos_y, -sin_y], axis=0)), split(kern_v)))
    kern_u = split(kern_u)
    ku_ref[...] = kern_u
    kh_ref[...] = kern_h
    vis_ref[...] = vis
    res_re, res_im = predict(columns, kern_u, kern_h, vis, scale)
    rows = grid_rows(res_re, res_im, kern_u, kern_h)
    own_ref[...] = rows
    for d in range(groups * count):
        rows_ref[height * d : height * (d + 1), :] = rows


def group_corner(corner_ref, near_refs, group, groups, index):
    refs = [corner_ref] + list(near_refs)
    back = (lax.axis_index("freq") - group) % groups
    value = refs[0][0, index]
    for k in range(1, groups):
        value = jnp.where(back == k, refs[k][0, index], value)
    return value


def second_kernel(
    all_ref, select_ref, own_ref, col_ref, ku_ref, kh_ref, vis_ref, back_ref, *, count, cap, groups, scale,
):
    lane_groups = LANES // cap
    height = col_ref.shape[0]
    total = groups * count
    chunk = math.gcd(total, 32)

    def overlap(part, carry):
        blocks = []
        for d in range(chunk):
            at = pl.multiple_of((part * chunk + d) * height, 8)
            blocks.append(split(all_ref[pl.ds(at, height), :]))
        at = pl.multiple_of(part * chunk * LANES, LANES)
        return carry + dot_nn(jnp.concatenate(blocks, axis=1), select_ref[pl.ds(at, chunk * LANES), :])

    extra = jnp.zeros((2 * height, LANES), F32)
    if total == chunk:
        extra = overlap(0, extra)
    else:
        extra = lax.fori_loop(0, total // chunk, overlap, extra)
    columns = col_ref[...] + (GAIN_STEP * scale * (GRID / 2)) * fold(extra)
    kern_u, kern_h = ku_ref[...], kh_ref[...]
    res_re, res_im = predict(columns, kern_u, kern_h, vis_ref[...], scale)
    rows = own_ref[...] + grid_rows(res_re, res_im, kern_u, kern_h)
    tiles = count // lane_groups
    res_re = jnp.concatenate([res_re[:, LANES * t : LANES * (t + 1)] for t in range(tiles)], axis=0)
    res_im = jnp.concatenate([res_im[:, LANES * t : LANES * (t + 1)] for t in range(tiles)], axis=0)
    low = iota((tiles, LANES), 1) < cap
    back = [
        jnp.where(low, turn(res_re, -j * cap), turn(res_im, (1 - j) * cap)) for j in range(lane_groups)
    ]
    for s in range(count):
        tile, j, down = s // lane_groups, s % lane_groups, s // ACROSS
        for g in range(groups):
            at = BACK * (g * count + s)
            back_ref[at : at + 8, :] = rows[8 * down : 8 * down + 8]
            back_ref[at + 8 : at + 9, :] = back[j][tile : tile + 1]


def prepare_kernel(*refs, count, groups):
    corner_ref, near_refs = refs[0], refs[1:groups]
    cos_ref, sin_ref, cos_x_ref, sin_x_ref, select_ref, freq_ref = refs[groups:]
    facet = lax.axis_index("facet")
    x_start = facet % ACROSS * FACET - GRID // 2
    u_start = corner_ref[0, facet]
    row, col = iota((LANES, LANES), 0), iota((LANES, LANES), 1)
    same = (row < SUB) == (col < SUB)
    row_a, col_a = row & (SUB - 1), col & (SUB - 1)
    behind = jnp.where(same, row_a - col_a, GRID)
    across = jnp.where(same, row_a + col_a, GRID)
    sign = jnp.where(col < SUB, 1.0, -1.0)
    half = GRID // 2

    def fill(d, carry):
        u_other = group_corner(corner_ref, near_refs, d // count, groups, d % count)
        freq_ref[pl.ds(d, 1), :] = jnp.full((1, LANES), u_other, I32)
        ahead = ((u_start - u_other + half) & (GRID - 1)) - half
        mirror = (-u_start - u_other) & (GRID - 1)
        select = jnp.where(behind == ahead, 1.0, 0.0) + jnp.where(across == mirror, sign, 0.0)
        select_ref[pl.ds(pl.multiple_of(d * LANES, LANES), LANES), :] = select.astype(BF16)
        return carry

    lax.fori_loop(0, groups * count, fill, 0)
    freq = freq_ref[...]
    cos_x, sin_x = phase_pair((freq + (iota(freq.shape, 1) & (SUB - 1))) * x_start)
    cos_x_ref[...] = cos_x
    sin_x_ref[...] = jnp.where(iota(freq.shape, 1) < SUB, -sin_x, sin_x)
    total = groups * count
    for at, cos_u, sin_u in phase_tiles(freq):
        place = slice(at // CHUNK * total, (at // CHUNK + 1) * total), slice(at % CHUNK, at % CHUNK + LANES)
        cos_ref[place] = cos_u
        sin_ref[place] = -sin_u


def image_kernel(
    got_ref, table_ref, cos_ref, sin_ref, cos_x_ref, sin_x_ref, hits_ref, rank_ref, image_ref,
    out_ref, res_ref, left_ref, *, count, groups, cap, scale,
):
    total = groups * count
    low = iota((FROWS, LANES), 1) < SUB
    cos_x, sin_x = cos_x_ref[...], sin_x_ref[...]
    for d in range(total):
        block = got_ref[BACK * d : BACK * d + 8, :]
        moved = block * cos_x[d : d + 1] + pltpu.roll(block, SUB, 1) * sin_x[d : d + 1]
        both = jnp.concatenate([jnp.where(low, moved, -moved), pltpu.roll(moved, SUB, 1)], axis=0)
        left_ref[16 * d : 16 * d + 16, :] = both.astype(BF16)
    for at in range(0, FACET, CHUNK):
        cut = slice(at, at + CHUNK)
        both = dot_nn(left_ref[...], table_ref[:, cut])
        dirty = jnp.zeros((FROWS, CHUNK), F32)
        for d in range(total):
            row = at // CHUNK * total + d
            dirty = dirty + both[16 * d : 16 * d + 8] * spread_row(cos_ref, row)
            dirty = dirty + both[16 * d + 8 : 16 * d + 16] * spread_row(sin_ref, row)
        out_ref[:, cut] = image_ref[:, cut] + (GAIN_STEP * scale) * dirty

    rows = rank_ref.shape[1]
    first = lax.axis_index("freq") * (count * BACK) + 8
    back = jnp.concatenate([got_ref[pl.ds(first + BACK * s, 1), :] for s in range(count)], axis=0)
    picked = []
    for part in range(2):
        place = (iota((LANES, rows), 0) == rank_ref[...] + part * cap).astype(F32)
        found = dot_nn(back, place, exact_products)
        picked.append(jnp.sum(found * hits_ref[...], axis=0, keepdims=True))
    res_ref[...] = jnp.concatenate(picked, axis=0)


def on_device(model_image, visibilities, kernel_u, kernel_v, owners, offsets, corners):
    count = lax.axis_size("facet")
    groups = lax.axis_size("freq")
    rows = owners.shape[0]
    cap = 4 * rows // count
    assert count % ACROSS == 0 and 2 * cap <= LANES and LANES % cap == 0
    scale = 1.0 / math.sqrt(count * FROWS * FACET)
    lane_groups, row_blocks, piece = layout_of(cap)
    height = count // ACROSS * FROWS
    slots = count * cap
    total = groups * count
    corner = corners[0].T
    owner_row = owners.reshape(1, rows)
    smem = pl.BlockSpec(memory_space=pltpu.SMEM)
    vmem = pl.BlockSpec(memory_space=pltpu.VMEM)
    far = pl.BlockSpec(memory_space=pltpu.HBM)
    params = pltpu.CompilerParams(vmem_limit_bytes=48 * 1024 * 1024)

    def shape(*dims, dtype=F32):
        return jax.ShapeDtypeStruct(dims, dtype)

    def call(body, out_shape, scalars, arrays, name, scratch=(), space=vmem, **sizes):
        return pl.pallas_call(
            lambda *refs: body(*refs, **sizes),
            out_shape=out_shape,
            in_specs=[smem] * len(scalars) + [space] * len(arrays),
            out_specs=jax.tree.map(lambda _: vmem, out_shape),
            scratch_shapes=scratch,
            compiler_params=params,
            name=name,
        )(*scalars, *arrays)

    def exchange(block, axes, parts):
        view = block.reshape(parts, 1, block.size // parts)
        return lax.all_to_all(view, axes, split_axis=0, concat_axis=0, tiled=True).reshape(block.shape)

    inputs = [corner, owner_row, visibilities, kernel_u, kernel_v, offsets, model_image]
    send, table, hits, rank, corner, start = call(
        send_kernel,
        (
            shape(count * piece, LANES),
            shape(2 * SUB, FACET, dtype=BF16),
            shape(count, rows),
            shape(1, rows, dtype=I32),
            shape(*corner.shape, dtype=I32),
            shape(8, LANES, dtype=I32),
        ),
        [],
        [pltpu.with_memory_space_constraint(x, pltpu.HBM) for x in inputs],
        "send_rows",
        [pltpu.SMEM(corner.shape, I32)]
        + [pltpu.VMEM(x.shape, x.dtype) for x in inputs[1:]]
        + [
            pltpu.VMEM((count, LANES), I32),
            pltpu.VMEM((count, FACET), F32),
            pltpu.VMEM((count, FACET), F32),
            pltpu.VMEM((16 * count, FACET), BF16),
            pltpu.SemaphoreType.DMA((8,)),
        ],
        far,
        count=count,
        cap=cap,
    )
    near = [
        lax.ppermute(corner, "freq", [(g, (g + k) % groups) for g in range(groups)])
        for k in range(1, groups)
    ]
    got = exchange(send, "facet", count)
    columns, kern_u, kern_h, vis, spread, own = call(
        first_kernel,
        (
            shape(height, LANES),
            shape(2 * SUB, slots, dtype=BF16),
            shape(2 * height, slots),
            shape(2, slots),
            shape(total * height, LANES),
            shape(height, LANES),
        ),
        [],
        [start, got],
        "first_cycle",
        count=count,
        cap=cap,
        groups=groups,
        scale=scale,
    )
    everyone = exchange(spread, ("freq", "facet"), total)
    *phases, select = call(
        prepare_kernel,
        (
            shape(FACET // CHUNK * total, CHUNK),
            shape(FACET // CHUNK * total, CHUNK),
            shape(total, LANES),
            shape(total, LANES),
            shape(total * LANES, LANES, dtype=BF16),
        ),
        [corner, *near],
        [],
        "prepare",
        [pltpu.VMEM((total, LANES), I32)],
        count=count,
        groups=groups,
    )
    back = call(
        second_kernel,
        shape(total * BACK, LANES),
        [],
        [everyone, select, own, columns, kern_u, kern_h, vis],
        "second_cycle",
        count=count,
        cap=cap,
        groups=groups,
        scale=scale,
    )
    returned = exchange(back, ("freq", "facet"), total)
    return call(
        image_kernel,
        (shape(FROWS, FACET), shape(2, rows)),
        [],
        [returned, table, *phases, hits, rank, model_image],
        "form_image",
        [pltpu.VMEM((16 * total, LANES), BF16)],
        count=count,
        groups=groups,
        cap=cap,
        scale=scale,
    )


def solution(mesh):
    return jax.shard_map(
        on_device,
        mesh=mesh,
        in_specs=(
            P("facet", None),
            P(None, ("freq", "facet")),
            P(None, ("freq", "facet")),
            P(None, ("freq", "facet")),
            P(("freq", "facet"), None),
            P(None, ("freq", "facet")),
            P("freq", None, None),
        ),
        out_specs=(P("facet", None), P(None, ("freq", "facet"))),
        check_vma=False,
    )
```

```python
import math

import jax
import jax.numpy as jnp
from jax import lax
from jax.experimental import pallas as pl
from jax.experimental.pallas import tpu as pltpu
from jax.sharding import PartitionSpec as P

GRID = 16384
FACET = 2048
FROWS = 8
SUB = 64
SUPPORT = 16
LANES = 128
ACROSS = GRID // FACET
GROUPS = 4
BACK = FROWS + 1
TURNS = FACET // LANES
GAIN_STEP = 0.5

F32 = jnp.float32
BF16 = jnp.bfloat16
I32 = jnp.int32
exact_products = lax.Precision.HIGHEST


def iota(shape, dim):
    return lax.broadcasted_iota(I32, shape, dim)


def phase_pair(index):
    moved = index + GRID // 8
    quadrant = (moved >> 12) & 3
    angle = ((moved & (GRID // 4 - 1)) - GRID // 8).astype(F32) * (2.0 * math.pi / GRID)
    sq = angle * angle
    sin_p = angle * (1.0 + sq * (-1.0 / 6 + sq * (1.0 / 120 + sq * (-1.0 / 5040 + sq * (1.0 / 362880)))))
    cos_p = 1.0 + sq * (-0.5 + sq * (1.0 / 24 + sq * (-1.0 / 720 + sq * (1.0 / 40320))))
    swap = (quadrant & 1) == 1
    cos_v = jnp.where(swap, sin_p, cos_p)
    sin_v = jnp.where(swap, cos_p, sin_p)
    cos_v = jnp.where((quadrant == 1) | (quadrant == 2), -cos_v, cos_v)
    sin_v = jnp.where(quadrant >= 2, -sin_v, sin_v)
    return cos_v, sin_v


def phase_tiles(freq):
    cos_v, sin_v = phase_pair(freq * iota(freq.shape, 1))
    turn_c, turn_s = phase_pair(freq * LANES)
    for tile in range(FACET // LANES):
        yield tile * LANES, cos_v, sin_v
        cos_v, sin_v = cos_v * turn_c - sin_v * turn_s, sin_v * turn_c + cos_v * turn_s


def dot_nt(left, right, precision=None):
    return lax.dot_general(
        left, right, (((1,), (1,)), ((), ())), precision=precision, preferred_element_type=F32
    )


def dot_nn(left, right, precision=None):
    return lax.dot_general(
        left, right, (((1,), (0,)), ((), ())), precision=precision, preferred_element_type=F32
    )


def split(value):
    high = value.astype(BF16)
    return jnp.concatenate([high, (value - high.astype(F32)).astype(BF16)], axis=0)


def fold(value):
    half = value.shape[0] // 2
    return value[:half] + value[half:]


def spread_row(ref, row):
    return ref[pl.ds(row, FROWS, stride=0), :]


def layout_of(cap):
    lane_groups = LANES // cap
    row_blocks = -(-GROUPS // min(lane_groups, GROUPS))
    return lane_groups, row_blocks, FROWS + 8 * row_blocks + 2


def turn(value, shift):
    shift = shift % LANES
    return pltpu.roll(value, shift, 1) if shift else value


def side_by_side(ref, height, half=None):
    starts = list(range(0, ref.shape[0], height))
    if half is not None:
        size = len(starts) // 2
        starts = starts[size * half : size * (half + 1)]
    return jnp.concatenate([ref[k : k + height, :] for k in starts], axis=1)


def slot_parts(owner_row, count):
    rows = owner_row.shape[1]
    hits = (iota((count, rows), 0) == owner_row).astype(F32)
    earlier = (iota((rows, rows), 0) < iota((rows, rows), 1)).astype(F32)
    before = dot_nn(hits.astype(BF16), earlier.astype(BF16))
    return hits, jnp.sum(before * hits, axis=0, keepdims=True).astype(I32)


def send_kernel(
    corner_hbm, owner_hbm, vis_hbm, ku_hbm, kv_hbm, off_hbm, image_hbm,
    send_ref, hits_ref, rank_ref, corner_out, start_ref,
    corner_ref, owner_ref, vis_ref, ku_ref, kv_ref, off_ref, image_ref,
    freq_ref, table_ref, mod_ref, sem_ref, *, count, cap,
):
    lane_groups, row_blocks, piece = layout_of(cap)
    sources = [corner_hbm, image_hbm, owner_hbm, vis_hbm, ku_hbm, kv_hbm, off_hbm, corner_hbm]
    targets = [corner_ref, image_ref, owner_ref, vis_ref, ku_ref, kv_ref, off_ref, corner_out]
    copies = [
        pltpu.make_async_copy(src, dst, sem_ref.at[i]) for i, (src, dst) in enumerate(zip(sources, targets))
    ]
    for copy in copies:
        copy.start()
    facet = lax.axis_index("facet")
    x_start = facet % ACROSS * FACET - GRID // 2
    for at, cos_t, sin_t in phase_tiles(iota((SUB, LANES), 0)):
        table_ref[at : at + SUB, :] = cos_t.astype(BF16)
        table_ref[at + SUB : at + LANES, :] = sin_t.astype(BF16)
    copies[0].wait()
    start_ref[...] = jnp.full(start_ref.shape, corner_ref[1, facet], I32)
    for s in range(count):
        freq_ref[s : s + 1, :] = jnp.full((1, LANES), corner_ref[0, s], I32)
    freq = freq_ref[...]
    for copy in copies[1:]:
        copy.wait()
    for at, cos_u, sin_u in phase_tiles(freq):
        for y in range(FROWS):
            row = jnp.broadcast_to(image_ref[y : y + 1, at : at + LANES], (count, LANES))
            start = 2 * count * (at // LANES * FROWS + y)
            mod_ref[start : start + count, :] = (row * cos_u).astype(BF16)
            mod_ref[start + count : start + 2 * count, :] = (row * -sin_u).astype(BF16)
    prod = dot_nt(side_by_side(mod_ref, 2 * FROWS * count), side_by_side(table_ref, LANES))
    low = iota(freq.shape, 1) < SUB
    cos_x, sin_x = phase_pair((freq + (iota(freq.shape, 1) & (SUB - 1))) * x_start)
    sin_x = jnp.where(low, sin_x, -sin_x)
    for y in range(FROWS):
        start = 2 * count * y
        real_p = prod[start : start + count]
        imag_p = pltpu.roll(prod[start + count : start + 2 * count], SUB, 1)
        col = jnp.where(low, real_p + imag_p, imag_p - real_p)
        send_ref[pl.ds(y, count, stride=piece), :] = col * cos_x + pltpu.roll(col, SUB, 1) * sin_x

    owner_row = owner_ref[...]
    rows = owner_row.shape[1]
    hits, rank = slot_parts(owner_row, count)
    hits_ref[...] = hits
    rank_ref[...] = rank
    place = [
        (iota((LANES, rows), 0) == rank + group * cap).astype(F32).astype(BF16)
        for group in range(max(2, GROUPS // row_blocks))
    ]
    high = 16 * -(-row_blocks // 2)
    taps = jnp.concatenate([ku_ref[...], kv_ref[...]], axis=0)
    left, places = [], []
    for group in range(GROUPS // row_blocks):
        mine = taps[8 * row_blocks * group : 8 * row_blocks * (group + 1)]
        if high > 8 * row_blocks:
            mine = jnp.concatenate([mine, jnp.zeros((high - 8 * row_blocks, rows), F32)], axis=0)
        both = split(mine)
        left += [both[:high], both[high:]]
        places += [place[group], place[group]]
    stacked = jnp.concatenate(left, axis=1)
    half_hits = jnp.concatenate([hits] * len(left), axis=1)
    masked = [
        stacked * jnp.broadcast_to(half_hits[s : s + 1], stacked.shape).astype(BF16) for s in range(count)
    ]
    total = dot_nt(jnp.concatenate(masked, axis=0), jnp.concatenate(places, axis=1))
    vis, offset = vis_ref[...], off_ref[...].astype(F32)
    vis = split(jnp.concatenate([hits * vis[0:1], hits * vis[1:2]], axis=0))
    offset = jnp.concatenate([hits * offset[0:1], hits * offset[1:2]], axis=0).astype(BF16)
    misc = jnp.concatenate([vis[: 2 * count], vis[2 * count :], offset], axis=1)
    misc = dot_nt(misc, jnp.concatenate([place[0], place[0], place[1]], axis=1))
    for s in range(count):
        at = piece * (s + 1) - 2
        send_ref[piece * s + FROWS : at, :] = total[high * s : high * s + 8 * row_blocks]
        send_ref[at : at + 1, :] = misc[s : s + 1]
        send_ref[at + 1 : at + 2, :] = misc[count + s : count + s + 1]


def place_kernel(taps, offset):
    low = jnp.concatenate([taps, jnp.zeros((8, LANES), F32)], axis=0)
    for step in (1, 2, 4):
        bit = jnp.broadcast_to((offset & step) != 0, low.shape)
        low = jnp.where(bit, pltpu.roll(low, step, 0), low)
    zero = jnp.zeros((8, LANES), F32)
    blocks = [low[0:8], low[8:16], low[16:24]]
    for step in (1, 2, 4):
        bit = jnp.broadcast_to((offset & (8 * step)) != 0, (8, LANES))
        size = min(len(blocks) + step, SUB // 8)
        wide = blocks + [zero] * (size - len(blocks))
        blocks = [jnp.where(bit, wide[k - step] if k >= step else zero, wide[k]) for k in range(size)]
    return jnp.concatenate(blocks, axis=0)


def predict(columns, kern_u, kern_h, vis, scale):
    height = columns.shape[0]
    low = iota(columns.shape, 1) < SUB
    turned = pltpu.roll(columns, SUB, 1)
    twice = jnp.concatenate([jnp.where(low, columns, turned), jnp.where(low, turned, columns)], axis=0)
    partial = fold(dot_nn(split(twice), kern_u))
    part_re, part_im = partial[:height], partial[height:]
    h_re, h_im = kern_h[:height], kern_h[height:]
    pred_re = jnp.sum(h_re * part_re - h_im * part_im, axis=0, keepdims=True)
    pred_im = jnp.sum(h_re * part_im + h_im * part_re, axis=0, keepdims=True)
    return vis[0:1] - scale * pred_re, vis[1:2] - scale * pred_im


def grid_rows(res_re, res_im, kern_u, kern_h):
    height = kern_h.shape[0] // 2
    h_re, h_im = kern_h[:height], kern_h[height:]
    weighted = jnp.concatenate([h_re * res_re + h_im * res_im, h_re * res_im - h_im * res_re], axis=0)
    rows = fold(dot_nt(split(weighted), kern_u))
    rows = rows + pltpu.roll(rows, SUB, 1)
    return jnp.where(iota((height, LANES), 1) < SUB, rows[:height], rows[height:])


def first_kernel(
    start_ref, got_ref, col_ref, ku_ref, kh_ref, vis_ref, rows_ref, own_ref, *, count, cap, groups, scale,
):
    lane_groups, row_blocks, piece = layout_of(cap)
    height = count // ACROSS * FROWS
    sums = []
    for down in range(count // ACROSS):
        total = got_ref[piece * down * ACROSS : piece * down * ACROSS + FROWS, :]
        for across in range(1, ACROSS):
            at = piece * (down * ACROSS + across)
            total = total + got_ref[at : at + FROWS, :]
        sums.append(total)
    columns = jnp.concatenate(sums, axis=0)
    col_ref[...] = columns
    lane_group = iota((8, LANES), 1) // cap
    u_list, v_list, vis_list = [], [], []
    for tile in range(count // lane_groups):
        found = [None] * (GROUPS + 2)
        for j in range(lane_groups):
            base = piece * (tile * lane_groups + j)
            moved = []
            for k in range(GROUPS):
                at = base + FROWS + 8 * (k % row_blocks)
                moved.append(turn(got_ref[at : at + 8, :], (j - k // row_blocks) * cap))
            misc = got_ref[base + piece - 2 : base + piece, :]
            moved += [turn(misc, j * cap), turn(misc, (j - 1) * cap)]
            for k, value in enumerate(moved):
                mine = lane_group[: value.shape[0]] == j
                found[k] = value if j == 0 else jnp.where(mine, value, found[k])
        offset = found[5].astype(I32)
        u_list.append(place_kernel(jnp.concatenate(found[0:2], axis=0), offset[0:1]))
        v_list.append(place_kernel(jnp.concatenate(found[2:4], axis=0), offset[1:2]))
        vis_list.append(found[4])
    kern_u = jnp.concatenate(u_list, axis=1)
    kern_v = jnp.concatenate(v_list, axis=1)
    vis = jnp.concatenate(vis_list, axis=1)
    row = iota((height, LANES), 0)
    y_pos = row // FROWS * FACET - GRID // 2 + row % FROWS
    cos_y, sin_y = phase_pair((start_ref[0:1, :] + (iota((height, LANES), 1) & (SUB - 1))) * y_pos)
    kern_h = fold(dot_nn(split(jnp.concatenate([cos_y, -sin_y], axis=0)), split(kern_v)))
    kern_u = split(kern_u)
    ku_ref[...] = kern_u
    kh_ref[...] = kern_h
    vis_ref[...] = vis
    res_re, res_im = predict(columns, kern_u, kern_h, vis, scale)
    rows = grid_rows(res_re, res_im, kern_u, kern_h)
    own_ref[...] = rows
    for d in range(groups * count):
        rows_ref[height * d : height * (d + 1), :] = rows


def group_corner(corner_ref, near_refs, group, groups, index):
    refs = [corner_ref] + list(near_refs)
    back = (lax.axis_index("freq") - group) % groups
    value = refs[0][0, index]
    for k in range(1, groups):
        value = jnp.where(back == k, refs[k][0, index], value)
    return value


def second_kernel(
    all_ref, select_ref, own_ref, col_ref, ku_ref, kh_ref, vis_ref, *rest, count, cap, groups, scale,
):
    back_ref = rest[-1]
    lane_groups = LANES // cap
    height = col_ref.shape[0]
    total = groups * count
    chunk = math.gcd(total, 32)

    def overlap(part, carry):
        blocks = []
        for d in range(chunk):
            at = pl.multiple_of((part * chunk + d) * height, 8)
            blocks.append(split(all_ref[pl.ds(at, height), :]))
        size = chunk // 2
        halves = []
        for half in range(2):
            at = pl.multiple_of((2 * part + half) * size * LANES, LANES)
            left = jnp.concatenate(blocks[size * half : size * (half + 1)], axis=1)
            halves.append(dot_nn(left, select_ref[pl.ds(at, size * LANES), :]))
        return carry + (halves[0] - halves[1])

    extra = jnp.zeros((2 * height, LANES), F32)
    if total == chunk:
        extra = overlap(0, extra)
    else:
        extra = lax.fori_loop(0, total // chunk, overlap, extra)
    columns = col_ref[...] + (GAIN_STEP * scale * (GRID / 2)) * fold(extra)
    kern_u, kern_h = ku_ref[...], kh_ref[...]
    res_re, res_im = predict(columns, kern_u, kern_h, vis_ref[...], scale)
    rows = own_ref[...] + grid_rows(res_re, res_im, kern_u, kern_h)
    tiles = count // lane_groups
    res_re = jnp.concatenate([res_re[:, LANES * t : LANES * (t + 1)] for t in range(tiles)], axis=0)
    res_im = jnp.concatenate([res_im[:, LANES * t : LANES * (t + 1)] for t in range(tiles)], axis=0)
    low = iota((tiles, LANES), 1) < cap
    back = [
        jnp.where(low, turn(res_re, -j * cap), turn(res_im, (1 - j) * cap)) for j in range(lane_groups)
    ]
    for s in range(count):
        tile, j, down = s // lane_groups, s % lane_groups, s // ACROSS
        for g in range(groups):
            at = BACK * (g * count + s)
            back_ref[at : at + 8, :] = rows[8 * down : 8 * down + 8]
            back_ref[at + 8 : at + 9, :] = back[j][tile : tile + 1]


def side_of(index, total):
    chunk = math.gcd(total, 32)
    return jnp.where(index % chunk < chunk // 2, 1.0, -1.0)


def in_eights(total, step):
    def eight(part, carry):
        for k in range(8):
            step(part * 8 + k)
        return carry

    lax.fori_loop(0, total // 8, eight, 0)


def select_kernel(*refs, count, groups):
    corner_ref, near_refs = refs[0], refs[1:groups]
    select_ref = refs[groups]
    u_start = corner_ref[0, lax.axis_index("facet")]
    row, col = iota((LANES, LANES), 0), iota((LANES, LANES), 1)
    same = (row < SUB) == (col < SUB)
    row_a, col_a = row & (SUB - 1), col & (SUB - 1)
    behind = jnp.where(same, row_a - col_a, GRID)
    across = jnp.where(same, row_a + col_a, GRID)
    sign = jnp.where(col < SUB, 1.0, -1.0)
    half = GRID // 2

    def fill(d):
        u_other = group_corner(corner_ref, near_refs, d // count, groups, d % count)
        ahead = ((u_start - u_other + half) & (GRID - 1)) - half
        mirror = (-u_start - u_other) & (GRID - 1)
        select = jnp.where(behind == ahead, 1.0, 0.0) + jnp.where(across == mirror, sign, 0.0)
        select = select * side_of(d, groups * count)
        select_ref[pl.ds(pl.multiple_of(d * LANES, LANES), LANES), :] = select.astype(BF16)

    in_eights(groups * count, fill)


def turn_kernel(*refs, count, groups):
    corner_ref, near_refs = refs[0], refs[1:groups]
    same_ref, cross_ref, table_ref, freq_ref = refs[groups:]
    total = groups * count
    x_start = lax.axis_index("facet") % ACROSS * FACET - GRID // 2
    cos_a, sin_a = phase_pair(iota((SUB, LANES), 0) * iota((SUB, LANES), 1))
    lane = iota((FROWS, LANES), 1)

    def fill(d):
        u_other = group_corner(corner_ref, near_refs, d // count, groups, d % count)
        freq_ref[pl.ds(d, 1), :] = jnp.full((1, LANES), u_other, I32)
        cos_u, sin_u = phase_pair(u_other * lane)
        cos_u, sin_u = [jnp.concatenate([x] * (SUB // FROWS), axis=0) for x in (cos_u, sin_u)]
        both = jnp.concatenate([cos_u * cos_a - sin_u * sin_a, -sin_u * cos_a - cos_u * sin_a], axis=0)
        table_ref[pl.ds(pl.multiple_of(d * LANES, LANES), LANES), :] = both.astype(BF16)

    in_eights(total, fill)
    freq = freq_ref[...] + (iota((total, LANES), 1) & (SUB - 1))
    low = iota((total, LANES), 1) < SUB
    cos_x, sin_x = phase_pair(freq * x_start)
    turn_c, turn_s = phase_pair(freq * LANES)
    side = side_of(iota((total, LANES), 0), total)
    cos_x, sin_x = cos_x * side, sin_x * side
    for h in range(TURNS):
        same_ref[pl.ds(h, total, stride=TURNS), :] = cos_x
        cross_ref[pl.ds(h, total, stride=TURNS), :] = jnp.where(low, -sin_x, sin_x)
        cos_x, sin_x = cos_x * turn_c - sin_x * turn_s, sin_x * turn_c + cos_x * turn_s


def image_kernel(
    got_ref, same_ref, cross_ref, table_ref, hits_ref, rank_ref, image_ref,
    out_ref, res_ref, flip_ref, left_ref, sum_ref, *, count, groups, cap, scale,
):
    total = groups * count
    chunk = math.gcd(total, 32)

    def gather(part, carry):
        for s in range(chunk):
            d = part * chunk + s
            block = got_ref[pl.ds(BACK * d, FROWS), :]
            flip_ref[FROWS * s : FROWS * (s + 1), :] = pltpu.roll(block, SUB, 1)
            near = pl.ds(pl.multiple_of(d * TURNS, TURNS), TURNS)
            same, cross = same_ref[near, :], cross_ref[near, :]
            for y in range(FROWS):
                straight = jnp.broadcast_to(block[y : y + 1], (FROWS, LANES))
                flipped = spread_row(flip_ref, FROWS * s + y)
                parts = [
                    straight * same[k : k + FROWS] + flipped * cross[k : k + FROWS]
                    for k in range(0, TURNS, FROWS)
                ]
                start = TURNS * (FROWS * s + y)
                left_ref[start : start + TURNS, :] = jnp.concatenate(parts, axis=0).astype(BF16)
        halves = []
        for half in range(2):
            size = chunk // 2 * LANES
            at = pl.multiple_of((2 * part + half) * size, LANES)
            left = side_by_side(left_ref, FROWS * TURNS, half)
            halves.append(dot_nn(left, table_ref[pl.ds(at, size), :]))
        return carry + (halves[0] - halves[1])

    dirty = jnp.zeros((FROWS * TURNS, LANES), F32)
    if total == chunk:
        dirty = gather(0, dirty)
    else:
        dirty = lax.fori_loop(0, total // chunk, gather, dirty)
    sum_ref[...] = dirty
    for h in range(TURNS):
        cut = slice(h * LANES, (h + 1) * LANES)
        out_ref[:, cut] = image_ref[:, cut] + (GAIN_STEP * scale) * sum_ref[pl.ds(h, FROWS, stride=TURNS), :]

    rows = rank_ref.shape[1]
    first = lax.axis_index("freq") * (count * BACK) + 8
    back = jnp.concatenate([got_ref[pl.ds(first + BACK * s, 1), :] for s in range(count)], axis=0)
    high = split(back)
    low = split(back - high[:count].astype(F32) - high[count:].astype(F32))
    back = jnp.concatenate([high, low[:count]], axis=0)
    picked = []
    for part in range(2):
        place = (iota((LANES, rows), 0) == rank_ref[...] + part * cap).astype(F32).astype(BF16)
        found = dot_nn(back, place)
        found = found[:count] + found[count : 2 * count] + found[2 * count :]
        picked.append(jnp.sum(found * hits_ref[...], axis=0, keepdims=True))
    res_ref[...] = jnp.concatenate(picked, axis=0)


def on_device(model_image, visibilities, kernel_u, kernel_v, owners, offsets, corners):
    count = lax.axis_size("facet")
    groups = lax.axis_size("freq")
    rows = owners.shape[0]
    cap = 4 * rows // count
    assert count % ACROSS == 0 and 2 * cap <= LANES and LANES % cap == 0
    scale = 1.0 / math.sqrt(count * FROWS * FACET)
    lane_groups, row_blocks, piece = layout_of(cap)
    height = count // ACROSS * FROWS
    slots = count * cap
    total = groups * count
    corner = corners[0].T
    owner_row = owners.reshape(1, rows)
    smem = pl.BlockSpec(memory_space=pltpu.SMEM)
    vmem = pl.BlockSpec(memory_space=pltpu.VMEM)
    far = pl.BlockSpec(memory_space=pltpu.HBM)
    params = pltpu.CompilerParams(vmem_limit_bytes=48 * 1024 * 1024)

    def shape(*dims, dtype=F32):
        return jax.ShapeDtypeStruct(dims, dtype)

    def call(body, out_shape, scalars, arrays, name, scratch=(), space=vmem, **sizes):
        return pl.pallas_call(
            lambda *refs: body(*refs, **sizes),
            out_shape=out_shape,
            in_specs=[smem] * len(scalars) + [space] * len(arrays),
            out_specs=jax.tree.map(lambda _: vmem, out_shape),
            scratch_shapes=scratch,
            compiler_params=params,
            name=name,
        )(*scalars, *arrays)

    def exchange(block, axes, parts):
        view = block.reshape(parts, 1, block.size // parts)
        return lax.all_to_all(view, axes, split_axis=0, concat_axis=0, tiled=True).reshape(block.shape)

    inputs = [corner, owner_row, visibilities, kernel_u, kernel_v, offsets, model_image]
    send, hits, rank, corner, start = call(
        send_kernel,
        (
            shape(count * piece, LANES),
            shape(count, rows),
            shape(1, rows, dtype=I32),
            shape(*corner.shape, dtype=I32),
            shape(8, LANES, dtype=I32),
        ),
        [],
        [pltpu.with_memory_space_constraint(x, pltpu.HBM) for x in inputs],
        "send_rows",
        [pltpu.SMEM(corner.shape, I32)]
        + [pltpu.VMEM(x.shape, x.dtype) for x in inputs[1:]]
        + [
            pltpu.VMEM((count, LANES), I32),
            pltpu.VMEM((FACET, LANES), BF16),
            pltpu.VMEM((2 * FROWS * count * TURNS, LANES), BF16),
            pltpu.SemaphoreType.DMA((8,)),
        ],
        far,
        count=count,
        cap=cap,
    )
    near = [
        lax.ppermute(corner, "freq", [(g, (g + k) % groups) for g in range(groups)])
        for k in range(1, groups)
    ]
    got = exchange(send, "facet", count)
    columns, kern_u, kern_h, vis, spread, own = call(
        first_kernel,
        (
            shape(height, LANES),
            shape(2 * SUB, slots, dtype=BF16),
            shape(2 * height, slots),
            shape(2, slots),
            shape(total * height, LANES),
            shape(height, LANES),
        ),
        [],
        [start, got],
        "first_cycle",
        count=count,
        cap=cap,
        groups=groups,
        scale=scale,
    )
    everyone = exchange(spread, ("freq", "facet"), total)
    select = call(
        select_kernel,
        shape(total * LANES, LANES, dtype=BF16),
        [corner, *near],
        [],
        "overlaps",
        count=count,
        groups=groups,
    )

    def make_turns(corner):
        return call(
            turn_kernel,
            (
                shape(total * TURNS, LANES),
                shape(total * TURNS, LANES),
                shape(total * LANES, LANES, dtype=BF16),
            ),
            [corner, *near],
            [],
            "turns",
            [pltpu.VMEM((total, LANES), I32)],
            count=count,
            groups=groups,
        )

    early = total <= 64
    turns = make_turns(corner) if early else ()
    back = call(
        second_kernel,
        shape(total * BACK, LANES),
        [],
        [everyone, select, own, columns, kern_u, kern_h, vis, *turns[:1]],
        "second_cycle",
        count=count,
        cap=cap,
        groups=groups,
        scale=scale,
    )
    if not early:
        back, corner = lax.optimization_barrier((back, corner))
        turns = make_turns(corner)
    returned = exchange(back, ("freq", "facet"), total)
    return call(
        image_kernel,
        (shape(FROWS, FACET), shape(2, rows)),
        [],
        [returned, *turns, hits, rank, model_image],
        "form_image",
        [
            pltpu.VMEM((FROWS * math.gcd(total, 32), LANES), F32),
            pltpu.VMEM((FROWS * TURNS * math.gcd(total, 32), LANES), BF16),
            pltpu.VMEM((FROWS * TURNS, LANES), F32),
        ],
        count=count,
        groups=groups,
        cap=cap,
        scale=scale,
    )


def solution(mesh):
    return jax.shard_map(
        on_device,
        mesh=mesh,
        in_specs=(
            P("facet", None),
            P(None, ("freq", "facet")),
            P(None, ("freq", "facet")),
            P(None, ("freq", "facet")),
            P(("freq", "facet"), None),
            P(None, ("freq", "facet")),
            P("freq", None, None),
        ),
        out_specs=(P("facet", None), P(None, ("freq", "facet"))),
        check_vma=False,
    )
```
